32 devices in a mesh: row: 4 (over y, x), col: 8 (over z, core).
Axes of the slice: x: 2, y: 2, z: 4, core: 2. Of those that a mesh axis runs over, the one named last changes fastest.
Arguments:
- tokens: bfloat16 [8192, 1024], P(('col', 'row')), may hold values from -6 to 6
- first_gain: float32 [1024], replicated, may hold values from 0.5 to 1.5
- query_weight: bfloat16 [1024, 1024], P('col', 'row'), may hold values from -0.1875 to 0.1875
- latent_weight: bfloat16 [1024, 512], P('col', 'row'), may hold values from -0.1875 to 0.1875
- key_weight: bfloat16 [256, 1024], P('col', 'row'), may hold values from -0.375 to 0.375
- value_weight: bfloat16 [256, 1024], P('col', 'row'), may hold values from -0.375 to 0.375
- output_weight: bfloat16 [1024, 1024], P('row', 'col'), may hold values from -3 to 3
- second_gain: float32 [1024], replicated, may hold values from 0.5 to 1.5
- gate_weight: bfloat16 [1024, 2816], P('col', 'row'), may hold values from -0.1875 to 0.1875
- up_weight: bfloat16 [1024, 2816], P('col', 'row'), may hold values from -0.1875 to 0.1875
- down_weight: bfloat16 [2816, 1024], P('row', 'col'), may hold values from -0.109375 to 0.109375
- block_order: int32 [8], replicated, may hold values from 0 to 7, as said below
- cotangent: bfloat16 [8192, 1024], P(('col', 'row')), may hold values from -6 to 6
Outputs:
- layer_output: float32 [8192, 1024], P(('col', 'row'))
- input_gradient: float32 [8192, 1024], P(('col', 'row'))
- first_gain_gradient: float32 [1024], replicated
- query_gradient: float32 [1024, 1024], P('col', 'row')
- latent_gradient: float32 [1024, 512], P('col', 'row')
- key_gradient: float32 [256, 1024], P('col', 'row')
- value_gradient: float32 [256, 1024], P('col', 'row')
- output_gradient: float32 [1024, 1024], P('row', 'col')
- second_gain_gradient: float32 [1024], replicated
- gate_gradient: float32 [1024, 2816], P('col', 'row')
- up_gradient: float32 [1024, 2816], P('col', 'row')
- down_gradient: float32 [2816, 1024], P('row', 'col')
The draws below stay inside these ranges and needn't reach their ends.
Inputs may be any that keep to these rules, and one draw needn't show every extreme that they name: Each value appears once; block c holds part block_order[c] % 8 of the prompt of group block_order[c] // 8; the 8 blocks of one group are the aligned run of blocks k * 8 to (k + 1) * 8 - 1 for some k.
All inputs are finite; a program needn't handle non-finite values.
Results may differ from the reference program's by a relative error of at most 0.024.
Values may be sent and summed in bfloat16 or wider, within the bound.
No kernel may reach another device: no remote copies, remote signals or barrier semaphores. Data moves between devices by JAX's collectives and lax.ppermute only.
A program may use at most 256 MiB of HBM per device.

```python
import jax
import jax.numpy as jnp
from jax import lax

D = 1024
HEADS = 16
HEAD_DIM = 64
LATENT_HEADS = 2
LATENT = 256
FF = 2816
PROMPT = 4096
CONT = 512
BLOCK = 1024
PORTION = 512
PORTIONS = 8
GROUPS = 1
TOKENS = 8192
N_COL = 8


def draw_block_order(key, part):
    run_key = jax.random.fold_in(key, 11)
    place_key = jax.random.fold_in(key, 23)
    run_groups = jax.random.permutation(run_key, GROUPS).astype(jnp.int32)
    place_keys = jax.random.split(place_key, GROUPS)
    places = jax.vmap(lambda single: jax.random.permutation(single, PORTIONS))(place_keys).astype(jnp.int32)
    order = run_groups[:, None] * PORTIONS + places
    return order.reshape(GROUPS * PORTIONS).astype(jnp.int32)


def block_levels(stream_key, extent, pieces, smallest, largest):
    factor_of = 1.0
    for dim, shards_of in pieces:
        draws = jax.random.uniform(jax.random.fold_in(jax.random.fold_in(stream_key, 6), dim), (shards_of,), jnp.float32, smallest / len(pieces), largest / len(pieces))
        factor_of = factor_of * jnp.repeat(jnp.exp(draws), extent[dim] // shards_of).reshape((-1,) + (1,) * (len(extent) - 1 - dim))
    return factor_of


def normal_values(own_key, shape, deviation, limit, cuts=(), held_as=jnp.bfloat16):
    entries = jax.random.normal(own_key, shape, jnp.float32) * deviation
    if len(cuts) > 0:
        entries = block_levels(own_key, shape, cuts, -0.22, 0.18) * entries
    return jnp.clip(entries, min=-limit, max=limit).astype(held_as)


def setup_inputs(seed: int = 0) -> dict:
    splits = jax.random.split(jax.random.key(seed), 14)
    tokens = normal_values(splits[0], (TOKENS, D), 1.0, 6.0, ((0, 32),))
    first_gain = jnp.clip(1.0 + 0.1 * jax.random.normal(splits[1], (D,), jnp.float32), 0.5, 1.5)
    query_weight = normal_values(splits[2], (D, HEADS * HEAD_DIM), D ** -0.5, 0.1875, ((0, 8), (1, 4)))
    latent_weight = normal_values(splits[3], (D, LATENT_HEADS * LATENT), D ** -0.5, 0.1875, ((0, 8), (1, 4)))
    key_weight = normal_values(splits[4], (LATENT, HEADS * HEAD_DIM), LATENT ** -0.5, 0.375, ((0, 8), (1, 4)))
    value_weight = normal_values(splits[5], (LATENT, HEADS * HEAD_DIM), LATENT ** -0.5, 0.375, ((0, 8), (1, 4)))
    output_weight = normal_values(splits[6], (HEADS * HEAD_DIM, D), 4 ** -0.5, 3.0, ((0, 4), (1, 8)))
    second_gain = jnp.clip(1.0 + 0.1 * jax.random.normal(splits[7], (D,), jnp.float32), 0.5, 1.5)
    gate_weight = normal_values(splits[8], (D, FF), D ** -0.5, 0.1875, ((0, 8), (1, 4)))
    up_weight = normal_values(splits[9], (D, FF), D ** -0.5, 0.1875, ((0, 8), (1, 4)))
    down_weight = normal_values(splits[10], (FF, D), FF ** -0.5, 0.109375, ((0, 4), (1, 8)))
    block_order = draw_block_order(jax.random.fold_in(splits[13], 71), 0)
    cotangent = normal_values(splits[12], (TOKENS, D), 1.0, 6.0, ((0, 32),))
    return dict(tokens=tokens, first_gain=first_gain, query_weight=query_weight, latent_weight=latent_weight, key_weight=key_weight, value_weight=value_weight, output_weight=output_weight, second_gain=second_gain, gate_weight=gate_weight, up_weight=up_weight, down_weight=down_weight, block_order=block_order, cotangent=cotangent)


@jax.custom_vjp
def low(v):
    return lax.optimization_barrier(v.astype(jnp.bfloat16)).astype(jnp.float32)

@jax.custom_vjp
def low_back(v):
    return v

def low_keep(v):
    return (low(v), None)

def low_pass(kept, grad):
    return (grad,)

def back_keep(v):
    return (v, None)

def back_low(kept, grad):
    return (low(grad),)
low.defvjp(low_keep, low_pass)
low_back.defvjp(back_keep, back_low)
epsilon = 1e-05
masked_value = -1e+30

def dense(left, right):
    return jnp.dot(left, right, precision=lax.Precision.HIGHEST, preferred_element_type=jnp.float32)

def rms_norm(rows, gain):
    return rows * lax.rsqrt(lax.optimization_barrier(jnp.mean(rows * rows, axis=-1, keepdims=True)) + epsilon) * gain

def up_heads(latent, weight):
    shaped = latent.reshape(TOKENS, LATENT_HEADS, LATENT)
    table = weight.reshape(LATENT, HEADS // LATENT_HEADS, LATENT_HEADS, HEAD_DIM)
    result = jnp.einsum('tgl,lagd->tagd', shaped, table, precision=lax.Precision.HIGHEST, preferred_element_type=jnp.float32)
    return result.reshape(TOKENS, HEADS * HEAD_DIM)

def layer_forward(block_order, tokens, first_gain, query_weight, latent_weight, key_weight, value_weight, output_weight, second_gain, gate_weight, up_weight, down_weight):
    normed = low(rms_norm(tokens, first_gain))
    queries = low_back(low(dense(normed, query_weight)))
    latent = low_back(low(dense(normed, latent_weight)))
    keys = low_back(low(up_heads(latent, key_weight)))
    values = low_back(low(up_heads(latent, value_weight)))
    inverse = jnp.zeros((N_COL,), jnp.int32).at[block_order].set(jnp.arange(N_COL, dtype=jnp.int32))
    scale = HEAD_DIM ** (-0.5)

    def attend_block(column):
        ident = block_order[column]
        group = ident // PORTIONS
        place = ident % PORTIONS
        start = (column * BLOCK).astype(jnp.int32)
        query_rows = lax.dynamic_slice_in_dim(queries, start, BLOCK, 0).reshape(BLOCK, HEADS, HEAD_DIM)
        key_parts = []
        value_parts = []
        for part in range(PORTIONS):
            source = (inverse[group * PORTIONS + part] * BLOCK).astype(jnp.int32)
            key_parts.append(lax.dynamic_slice_in_dim(keys, source, PORTION, 0))
            value_parts.append(lax.dynamic_slice_in_dim(values, source, PORTION, 0))
        own = (start + PORTION).astype(jnp.int32)
        key_parts.append(lax.dynamic_slice_in_dim(keys, own, PORTION, 0))
        value_parts.append(lax.dynamic_slice_in_dim(values, own, PORTION, 0))
        key_rows = jnp.concatenate(key_parts, axis=0).reshape(PROMPT + PORTION, HEADS, HEAD_DIM)
        value_rows = jnp.concatenate(value_parts, axis=0).reshape(PROMPT + PORTION, HEADS, HEAD_DIM)
        scores = jnp.einsum('qhd,khd->hqk', query_rows, key_rows, precision=lax.Precision.HIGHEST, preferred_element_type=jnp.float32) * scale
        scores = low_back(scores)
        rows = jnp.arange(BLOCK, dtype=jnp.int32)[:, None]
        cols = jnp.arange(PROMPT + PORTION, dtype=jnp.int32)[None, :]
        following = rows >= PORTION
        later = rows - PORTION
        local_cols = cols - PROMPT
        prompt_ok = following | (cols <= place * PORTION + rows)
        local_ok = following & (later // CONT == local_cols // CONT) & (local_cols <= later) & (local_cols >= 0)
        allowed = jnp.where(cols < PROMPT, prompt_ok, local_ok)
        masked = jnp.where(allowed[None], scores, masked_value)
        total = jax.nn.logsumexp(masked, axis=-1, keepdims=True)
        probs = low(jnp.exp(masked - total))
        result = jnp.einsum('hqk,khd->qhd', probs, value_rows, precision=lax.Precision.HIGHEST, preferred_element_type=jnp.float32)
        return result.reshape(BLOCK, HEADS * HEAD_DIM)
    attended = lax.map(jax.checkpoint(attend_block), jnp.arange(N_COL, dtype=jnp.int32))
    attended = low_back(low(attended.reshape(TOKENS, HEADS * HEAD_DIM)))
    hidden = tokens + low_back(dense(attended, output_weight))
    normed2 = low(rms_norm(hidden, second_gain))
    gate = low_back(dense(normed2, gate_weight))
    up = low_back(dense(normed2, up_weight))
    act = low(jax.nn.silu(gate) * up)
    return hidden + low_back(dense(act, down_weight))

def reference(tokens, first_gain, query_weight, latent_weight, key_weight, value_weight, output_weight, second_gain, gate_weight, up_weight, down_weight, block_order, cotangent):
    floats = (tokens, first_gain, query_weight, latent_weight, key_weight, value_weight, output_weight, second_gain, gate_weight, up_weight, down_weight)
    floats = tuple((item.astype(jnp.float32) for item in floats))

    def bound(*items):
        return layer_forward(block_order, *items)
    layer_output, pullback = jax.vjp(bound, *floats)
    grads = pullback(cotangent.astype(jnp.float32))
    return (layer_output, grads[0], grads[1], grads[2], grads[3], grads[4], grads[5], grads[6], grads[7], grads[8], grads[9], grads[10])
```

```python
import functools

import jax
import jax.numpy as jnp
from jax import lax
from jax.experimental import pallas as pl
from jax.experimental.pallas import tpu as pltpu
from jax.sharding import PartitionSpec as P

HEAD_DIM = 64
LATENT_HEADS = 2
LATENT = 256
PROMPT = 4096
CONT = 512
KEY_TILE = 512
ROW_TILE = 256

epsilon = 1e-05
masked_value = -1e30
BF16 = jnp.bfloat16
F32 = jnp.float32


def dot(left, right, left_dim, right_dim):
    return lax.dot_general(
        left, right, (((left_dim,), (right_dim,)), ((), ())), preferred_element_type=F32
    )


def norm_forward(rows, gain):
    scale = lax.rsqrt(jnp.mean(rows * rows, axis=-1, keepdims=True) + epsilon)
    return (rows * scale * gain, scale)


def norm_backward(rows, scale, gain, grad_out):
    normal = rows * scale
    gain_term = jnp.sum(grad_out * normal, axis=0)
    inner = grad_out * gain
    grad_rows = scale * (inner - normal * jnp.mean(inner * normal, axis=-1, keepdims=True))
    return (grad_rows, gain_term)


def exchange(block, mask):
    return lax.ppermute(block, "row", [(i, i ^ mask) for i in range(lax.axis_size("row"))])


def gather_pieces(rows):
    half = rows.shape[0] // 2
    low, high = rows[:half], rows[half:]
    low_x = exchange(low, 1)
    high_y = exchange(high, 2)
    low_y = exchange(jnp.concatenate([low, low_x], axis=0), 2)
    high_x = exchange(jnp.concatenate([high, high_y], axis=0), 1)
    return [
        (low, high),
        (low_x, high_x[:half]),
        (low_y[:half], high_y),
        (low_y[half:], high_x[half:]),
    ]


def gather_near(rows):
    if lax.axis_size("row") != 4:
        return lax.all_gather(rows, "row", axis=0, tiled=True)
    return jnp.concatenate([part for piece in gather_pieces(rows) for part in piece], axis=0)


def gather_true(rows):
    if lax.axis_size("row") != 4:
        return lax.all_gather(rows, "row", axis=0, tiled=True)
    count = rows.shape[0]
    here = lax.axis_index("row")
    whole = jnp.zeros((4 * count,) + rows.shape[1:], rows.dtype)
    for j, piece in enumerate(gather_pieces(rows)):
        whole = lax.dynamic_update_slice_in_dim(
            whole, jnp.concatenate(piece, axis=0), (here ^ j) * count, 0
        )
    return whole


def scatter_pieces(pieces):
    half = pieces[0].shape[0] // 2
    low = [piece[:half] for piece in pieces]
    high = [piece[half:] for piece in pieces]
    low_in = exchange(jnp.concatenate([low[2], low[3]], axis=0), 2)
    high_in = exchange(jnp.concatenate([high[1], high[3]], axis=0), 1)
    low_on = (low[1].astype(F32) + low_in[half:].astype(F32)).astype(BF16)
    high_on = (high[2].astype(F32) + high_in[half:].astype(F32)).astype(BF16)
    low_last = exchange(low_on, 1)
    high_last = exchange(high_on, 2)
    low_sum = low[0].astype(F32) + low_in[:half].astype(F32) + low_last.astype(F32)
    high_sum = high[0].astype(F32) + high_in[:half].astype(F32) + high_last.astype(F32)
    return jnp.concatenate([low_sum, high_sum], axis=0)


def scatter_near(part):
    part = part.astype(BF16)
    if lax.axis_size("row") != 4:
        return lax.psum_scatter(part, "row", scatter_dimension=0, tiled=True).astype(F32)
    count = part.shape[0] // 4
    return scatter_pieces([part[j * count : (j + 1) * count] for j in range(4)])


def scatter_true(part):
    part = part.astype(BF16)
    if lax.axis_size("row") != 4:
        return lax.psum_scatter(part, "row", scatter_dimension=0, tiled=True).astype(F32)
    count = part.shape[0] // 4
    here = lax.axis_index("row")
    return scatter_pieces(
        [lax.dynamic_slice_in_dim(part, (here ^ j) * count, count, 0) for j in range(4)]
    )


def gather_features(part):
    if lax.axis_size("row") != 4:
        return lax.all_gather(part, "row", axis=1, tiled=True)
    count = part.shape[0]
    whole = gather_true(part)
    return jnp.concatenate([whole[j * count : (j + 1) * count] for j in range(4)], axis=1)


def scatter_features(part):
    part = part.astype(BF16)
    size = lax.axis_size("row")
    if size != 4:
        return lax.psum_scatter(part, "row", scatter_dimension=1, tiled=True)
    width = part.shape[1] // size
    stacked = jnp.concatenate([part[:, j * width : (j + 1) * width] for j in range(size)], axis=0)
    return scatter_true(stacked).astype(BF16)


def all_sum(value):
    for axis in ("row", "col"):
        size = lax.axis_size(axis)
        if size & (size - 1):
            value = lax.psum(value, axis)
            continue
        bit = 1
        while bit < size:
            value = value + lax.ppermute(value, axis, [(i, i ^ bit) for i in range(size)])
            bit *= 2
    return value


def masked_heads(tile, heads):
    lanes = lax.broadcasted_iota(jnp.int32, tile.shape, 1) // HEAD_DIM
    return [jnp.where(lanes == h, tile, jnp.zeros_like(tile)) for h in range(heads)]


def one_head(ref, h, rows):
    pair = pl.ds((h // 2) * 2 * HEAD_DIM, 2 * HEAD_DIM)
    own = ref[h * HEAD_DIM : (h + 1) * HEAD_DIM, rows]
    none = jnp.zeros_like(own)
    return pair, jnp.concatenate([own, none] if h % 2 == 0 else [none, own], axis=0)


def visit_tiles(meta, step, prompt_tiles, portion, rows, body):
    place = meta[prompt_tiles]
    first_rows = portion // ROW_TILE

    def visit(index, carry):
        is_prompt = index < first_rows
        row0 = index * ROW_TILE
        position = place * portion + row0
        later = row0 - portion
        key0 = step * KEY_TILE
        on_prompt = step < prompt_tiles
        prompt_full = is_prompt & on_prompt & (key0 + KEY_TILE - 1 <= position)
        prompt_part = is_prompt & on_prompt & (key0 <= position + ROW_TILE - 1)
        full = prompt_full | (jnp.logical_not(is_prompt) & on_prompt)
        own_part = (
            jnp.logical_not(is_prompt)
            & jnp.logical_not(on_prompt)
            & (later // CONT == step - prompt_tiles)
        )
        partly = (prompt_part & jnp.logical_not(prompt_full)) | own_part
        ahead = jnp.where(is_prompt, position - key0, later % CONT)

        @pl.when(full)
        def _():
            body(index, None)

        @pl.when(partly)
        def _():
            body(index, ahead)

        return carry

    lax.fori_loop(0, rows // ROW_TILE, visit, 0)


def hide(scores, ahead):
    if ahead is None:
        return scores
    key = lax.broadcasted_iota(jnp.int32, scores.shape, 0)
    query = lax.broadcasted_iota(jnp.int32, scores.shape, 1)
    return jnp.where(key <= query + ahead, scores, masked_value)


def attend_kernel(
    meta, q_t, key_in, value_in, key_own, value_own, out, out_low, lse, keys, values_t, acc, top, total,
    *, heads, prompt_tiles, portion, rows,
):
    step = pl.program_id(0)

    @pl.when(step == 0)
    def _():
        acc[...] = jnp.zeros_like(acc)
        top[...] = jnp.full_like(top, masked_value)
        total[...] = jnp.zeros_like(total)

    @pl.when(step < prompt_tiles)
    def _():
        keys[...] = key_in[...]
        values_t[...] = value_in[...].T

    @pl.when(step >= prompt_tiles)
    def _():
        keys[...] = key_own[...]
        values_t[...] = value_own[...].T

    def body(index, ahead):
        at = pl.ds(pl.multiple_of(index * ROW_TILE, ROW_TILE), ROW_TILE)
        for h in range(heads):
            pair, query = one_head(q_t, h, at)
            scores = hide(dot(keys[:, pair], query, 1, 0), ahead)
            before = top[h : h + 1, at]
            now = jnp.maximum(before, jnp.max(scores, axis=0, keepdims=True))
            probs = jnp.exp(scores - now)
            decay = jnp.exp(before - now)
            top[h : h + 1, at] = now
            total[h : h + 1, at] = decay * total[h : h + 1, at] + jnp.sum(
                probs, axis=0, keepdims=True
            )
            mine = slice(h * HEAD_DIM, (h + 1) * HEAD_DIM)
            acc[mine, at] = decay * acc[mine, at] + dot(values_t[mine, :], probs.astype(BF16), 1, 0)

    visit_tiles(meta, step, prompt_tiles, portion, rows, body)

    @pl.when(step == pl.num_programs(0) - 1)
    def _():
        lse[...] = top[...] + jnp.log(jnp.maximum(total[...], 1e-37))
        for h in range(heads):
            mine = slice(h * HEAD_DIM, (h + 1) * HEAD_DIM)
            result = acc[mine, :] / total[h : h + 1, :]
            out[mine, :] = result
            out_low[mine, :] = result.astype(BF16)


def attend_back_kernel(
    meta, q_t, grad_t, q, grad, lse, inner, key_in, value_in, key_own, value_own,
    query_grad, prompt_grad, own_grad,
    keys, keys_t, values, queries_apart, grads_apart, query_acc, key_acc, value_acc,
    *, heads, prompt_tiles, portion, rows,
):
    step = pl.program_id(0)
    wide = heads * ROW_TILE

    @pl.when(step == 0)
    def _():
        query_acc[...] = jnp.zeros_like(query_acc)

        def spread(index, carry):
            at = pl.ds(pl.multiple_of(index * ROW_TILE, ROW_TILE), ROW_TILE)
            far = pl.ds(pl.multiple_of(index * wide, wide), wide)
            queries_apart[far, :] = jnp.concatenate(masked_heads(q[at, :], heads), axis=0)
            grads_apart[far, :] = jnp.concatenate(masked_heads(grad[at, :], heads), axis=0)
            return carry

        lax.fori_loop(0, rows // ROW_TILE, spread, 0)

    key_acc[...] = jnp.zeros_like(key_acc)
    value_acc[...] = jnp.zeros_like(value_acc)

    @pl.when(step < prompt_tiles)
    def _():
        keys[...] = key_in[...]
        keys_t[...] = key_in[...].T
        values[...] = value_in[...]

    @pl.when(step >= prompt_tiles)
    def _():
        keys[...] = key_own[...]
        keys_t[...] = key_own[...].T
        values[...] = value_own[...]

    def body(index, ahead):
        at = pl.ds(pl.multiple_of(index * ROW_TILE, ROW_TILE), ROW_TILE)
        far = pl.ds(pl.multiple_of(index * wide, wide), wide)
        all_probs = []
        all_grads = []
        for h in range(heads):
            pair, query = one_head(q_t, h, at)
            _, out_grad = one_head(grad_t, h, at)
            scores = hide(dot(keys[:, pair], query, 1, 0), ahead)
            probs = jnp.exp(scores - lse[h : h + 1, at])
            dprobs = dot(values[:, pair], out_grad, 1, 0)
            score_grad = (probs * (dprobs - inner[h : h + 1, at])).astype(BF16)
            mine = slice(h * HEAD_DIM, (h + 1) * HEAD_DIM)
            query_acc[mine, at] += dot(keys_t[mine, :], score_grad, 1, 0)
            all_probs.append(probs.astype(BF16))
            all_grads.append(score_grad)
        value_acc[...] += dot(jnp.concatenate(all_probs, axis=1), grads_apart[far, :], 1, 0)
        key_acc[...] += dot(jnp.concatenate(all_grads, axis=1), queries_apart[far, :], 1, 0)

    visit_tiles(meta, step, prompt_tiles, portion, rows, body)

    width = heads * HEAD_DIM

    @pl.when(step < prompt_tiles)
    def _():
        prompt_grad[:, :width] = key_acc[...].astype(BF16)
        prompt_grad[:, width:] = value_acc[...].astype(BF16)

    @pl.when(step >= prompt_tiles)
    def _():
        own_grad[:, :width] = key_acc[...].astype(BF16)
        own_grad[:, width:] = value_acc[...].astype(BF16)

    @pl.when(step == pl.num_programs(0) - 1)
    def _():
        query_grad[...] = (query_acc[...] * HEAD_DIM**-0.5).astype(BF16)


def whole_spec(shape):
    return pl.BlockSpec(shape, lambda step, meta: (0, 0))


def attention_specs(width, prompt_tiles):
    def prompt_map(column):
        return lambda step, meta: (meta[jnp.minimum(step, prompt_tiles - 1)], column)

    def own_map(column):
        return lambda step, meta: (jnp.maximum(step - prompt_tiles, 0), column)

    tile = (KEY_TILE, width)
    return [
        pl.BlockSpec(tile, prompt_map(0)),
        pl.BlockSpec(tile, prompt_map(1)),
        pl.BlockSpec(tile, own_map(0)),
        pl.BlockSpec(tile, own_map(1)),
    ]


def attend(meta, q_t, prompt, own):
    width, rows = q_t.shape
    heads = width // HEAD_DIM
    portion = own.shape[0]
    prompt_tiles = PROMPT // KEY_TILE
    steps = prompt_tiles + portion // KEY_TILE
    keys = (prompt.shape[0] + portion) * rows * heads * 3 // 4
    return pl.pallas_call(
        functools.partial(
            attend_kernel, heads=heads, prompt_tiles=prompt_tiles, portion=portion, rows=rows
        ),
        grid_spec=pltpu.PrefetchScalarGridSpec(
            num_scalar_prefetch=1,
            grid=(steps,),
            in_specs=[whole_spec((width, rows))] + attention_specs(width, prompt_tiles),
            out_specs=[
                whole_spec((width, rows)),
                whole_spec((width, rows)),
                whole_spec((8, rows)),
            ],
            scratch_shapes=[
                pltpu.VMEM((KEY_TILE, width), BF16),
                pltpu.VMEM((width, KEY_TILE), BF16),
                pltpu.VMEM((width, rows), F32),
                pltpu.VMEM((8, rows), F32),
                pltpu.VMEM((8, rows), F32),
            ],
        ),
        out_shape=[
            jax.ShapeDtypeStruct((width, rows), F32),
            jax.ShapeDtypeStruct((width, rows), BF16),
            jax.ShapeDtypeStruct((8, rows), F32),
        ],
        compiler_params=pltpu.CompilerParams(dimension_semantics=("arbitrary",)),
        cost_estimate=pl.CostEstimate(
            flops=keys * HEAD_DIM * 16, transcendentals=keys, bytes_accessed=8 << 20
        ),
        name="attend",
    )(meta, q_t, prompt, prompt, own, own)


def attend_back(meta, q_t, grad_t, q, grad, lse, inner, prompt, own):
    width, rows = q_t.shape
    heads = width // HEAD_DIM
    portion = own.shape[0]
    prompt_tiles = PROMPT // KEY_TILE
    steps = prompt_tiles + portion // KEY_TILE
    keys = (prompt.shape[0] + portion) * rows * heads * 3 // 4
    tall = heads * rows
    return pl.pallas_call(
        functools.partial(
            attend_back_kernel, heads=heads, prompt_tiles=prompt_tiles, portion=portion, rows=rows
        ),
        grid_spec=pltpu.PrefetchScalarGridSpec(
            num_scalar_prefetch=1,
            grid=(steps,),
            in_specs=[
                whole_spec((width, rows)),
                whole_spec((width, rows)),
                whole_spec((rows, width)),
                whole_spec((rows, width)),
                whole_spec((8, rows)),
                whole_spec((8, rows)),
            ]
            + attention_specs(width, prompt_tiles),
            out_specs=[
                whole_spec((width, rows)),
                pl.BlockSpec(
                    (KEY_TILE, 2 * width),
                    lambda step, meta: (meta[jnp.minimum(step, prompt_tiles - 1)], 0),
                ),
                pl.BlockSpec(
                    (KEY_TILE, 2 * width),
                    lambda step, meta: (jnp.maximum(step - prompt_tiles, 0), 0),
                ),
            ],
            scratch_shapes=[
                pltpu.VMEM((KEY_TILE, width), BF16),
                pltpu.VMEM((width, KEY_TILE), BF16),
                pltpu.VMEM((KEY_TILE, width), BF16),
                pltpu.VMEM((tall, width), BF16),
                pltpu.VMEM((tall, width), BF16),
                pltpu.VMEM((width, rows), F32),
                pltpu.VMEM((KEY_TILE, width), F32),
                pltpu.VMEM((KEY_TILE, width), F32),
            ],
        ),
        out_shape=[
            jax.ShapeDtypeStruct((width, rows), BF16),
            jax.ShapeDtypeStruct((PROMPT, 2 * width), BF16),
            jax.ShapeDtypeStruct((portion, 2 * width), BF16),
        ],
        compiler_params=pltpu.CompilerParams(dimension_semantics=("arbitrary",)),
        cost_estimate=pl.CostEstimate(
            flops=keys * HEAD_DIM * 40, transcendentals=keys, bytes_accessed=14 << 20
        ),
        name="attend_back",
    )(meta, q_t, grad_t, q, grad, lse, inner, prompt, prompt, own, own)


def key_layout(block_order, portion):
    portions = PROMPT // portion
    column = lax.axis_index("col")
    base = column // portions * portions
    ident = block_order[column]
    group = ident // portions
    place = ident % portions
    slots = jnp.arange(block_order.shape[0], dtype=jnp.int32)
    parts = group * portions + jnp.arange(portions, dtype=jnp.int32)
    sources = jnp.sum(jnp.where(block_order[None, :] == parts[:, None], slots[None, :], 0), axis=1)
    split = portion // KEY_TILE
    tiles = (sources - base)[:, None] * split + jnp.arange(split, dtype=jnp.int32)[None, :]
    return jnp.concatenate([tiles.reshape(-1), place[None]]).astype(jnp.int32)


def bit_of(value, bit):
    return value // (1 << bit) % 2


def swapped(block, axis, distance):
    size = lax.axis_size(axis)
    return lax.ppermute(block, axis, [(i, i ^ 1 << distance) for i in range(size)])


def gather_prompt(held):
    portion = held.shape[0]
    portions = PROMPT // portion
    if portions == lax.axis_size("col"):
        return lax.all_gather(held, "col", axis=0, tiled=True)
    column = lax.axis_index("col")
    for bit in range(portions.bit_length() - 1):
        other = swapped(held, "col", bit)
        upper = bit_of(column, bit) == 1
        held = jnp.where(
            upper, jnp.concatenate([other, held], axis=0), jnp.concatenate([held, other], axis=0)
        )
    return held


def scatter_prompt(buffer, portion):
    portions = PROMPT // portion
    if portions == lax.axis_size("col"):
        return lax.psum_scatter(buffer, "col", scatter_dimension=0, tiled=True)
    column = lax.axis_index("col")
    for bit in reversed(range(portions.bit_length() - 1)):
        half = buffer.shape[0] // 2
        upper = bit_of(column, bit) == 1
        keep = jnp.where(upper, buffer[half:], buffer[:half])
        outgoing = jnp.where(upper, buffer[:half], buffer[half:])
        got = swapped(outgoing, "col", bit)
        buffer = (keep.astype(F32) + got.astype(F32)).astype(BF16)
    return buffer


def padded(block, width):
    return jnp.pad(block, ((0, 0), (0, width - block.shape[1])))


def to_strips(block, rows):
    count = block.shape[0]
    strips = [block[:, i : i + 128] for i in range(0, block.shape[1], 128)]
    tall = jnp.concatenate(strips, axis=0)
    return jnp.concatenate(
        [tall[i : i + rows] for i in range(0, tall.shape[0], rows)], axis=1
    ) if tall.shape[0] != rows else tall


def head_mask(width):
    group = lax.broadcasted_iota(jnp.int32, (LATENT_HEADS * LATENT, 2 * width), 0) // LATENT
    head = lax.broadcasted_iota(jnp.int32, (LATENT_HEADS * LATENT, 2 * width), 1) // HEAD_DIM
    return group == head % LATENT_HEADS


def per_device(
    tokens, first_gain, query_weight, latent_weight, key_weight, value_weight, output_weight,
    second_gain, gate_weight, up_weight, down_weight, block_order, cotangent,
):
    columns = lax.axis_size("col")
    share = query_weight.shape[0]
    width = query_weight.shape[1]
    features = latent_weight.shape[1]
    hidden_units = gate_weight.shape[1]
    units = -(-hidden_units // 128) * 128

    early = jnp.concatenate(
        [query_weight, latent_weight, output_weight.T], axis=1
    )
    pair_weight = jnp.concatenate([key_weight, value_weight], axis=1)
    late = jnp.concatenate(
        [padded(gate_weight, units), padded(up_weight, units), padded(down_weight.T, units)], axis=1
    )
    pair_rows = pair_weight.shape[0]
    strips = 2 * width // 128
    pair_flat = jnp.concatenate(
        [pair_weight[:, i * 128 : (i + 1) * 128] for i in range(strips)], axis=0
    )
    if pair_flat.shape[0] == share:
        early_all = lax.all_gather(
            jnp.concatenate([early, pair_flat], axis=1), "col", axis=0, tiled=True
        )
        flat_all = early_all[:, early.shape[1] :].reshape(columns, strips, pair_rows, 128)
    else:
        early_all = lax.all_gather(early, "col", axis=0, tiled=True)
        flat_all = lax.all_gather(pair_flat, "col", axis=0, tiled=True).reshape(
            columns, strips, pair_rows, 128
        )
    pair_full = jnp.concatenate(
        [flat_all[:, i].reshape(columns * pair_rows, 128) for i in range(strips)], axis=1
    )
    query_full = early_all[:, :width]
    latent_full = early_all[:, width : width + features]
    output_full = early_all[:, width + features : 2 * width + features]

    rows = tokens.astype(F32)
    normed, first_scale = norm_forward(rows, first_gain)
    normed_block = gather_true(normed.astype(BF16))
    block = normed_block.shape[0]
    portion = block // 2
    mask = head_mask(width)
    spread = jnp.where(mask, jnp.concatenate([pair_full] * LATENT_HEADS, axis=0), jnp.zeros((), BF16))
    latent_part = dot(normed_block, latent_full, 1, 0).astype(BF16)
    latent_all = gather_features(latent_part)
    pairs = dot(latent_all, spread, 1, 0).astype(BF16)
    own = pairs[portion:]
    prompt = gather_prompt(pairs[:portion])
    scale = HEAD_DIM**-0.5
    queries_t = (dot(query_full, normed_block, 0, 1).astype(BF16) * scale).astype(BF16)
    queries = (dot(normed_block, query_full, 1, 0).astype(BF16) * scale).astype(BF16)
    meta = key_layout(block_order, portion)
    late, prompt_first = lax.optimization_barrier((late, prompt[:8]))
    late_all = lax.all_gather(late, "col", axis=0, tiled=True)
    wide_full = late_all[:, : 2 * units]
    down_full = late_all[:, 2 * units :]
    cot_block = gather_near(cotangent)
    result_t, attended_t, lse = attend(meta, queries_t, prompt, own)
    branch = dot(attended_t, output_full, 0, 1)
    hidden = rows + scatter_true(branch)

    normed2, second_scale = norm_forward(hidden, second_gain)
    normed2_block = gather_near(normed2.astype(BF16))
    both = dot(normed2_block, wide_full, 1, 0)
    gate = both[:, :units]
    up = both[:, units:]
    sigma = jax.nn.sigmoid(gate)
    act = (gate * sigma * up).astype(BF16)
    act_grad = dot(cot_block, down_full, 1, 0)
    gate_grad = (act_grad * up * sigma * (1.0 + gate * (1.0 - sigma))).astype(BF16)
    up_grad = (act_grad * gate * sigma).astype(BF16)
    both_grad = jnp.concatenate([gate_grad, up_grad], axis=1)
    normed2_grad = scatter_near(dot(both_grad, wide_full, 1, 1))
    layer = hidden + scatter_near(dot(act, down_full, 1, 1))
    late_terms = jnp.concatenate(
        [
            dot(normed2_block, both_grad, 0, 0).astype(BF16),
            dot(cot_block, act, 0, 0).astype(BF16),
        ],
        axis=1,
    )
    late_sums = lax.psum_scatter(late_terms, "col", scatter_dimension=0, tiled=True).astype(F32)
    norm2_grad, second_gain_term = norm_backward(hidden, second_scale, second_gain, normed2_grad)
    hidden_grad = cotangent.astype(F32) + norm2_grad

    branch_block = gather_true(hidden_grad.astype(BF16))
    attended_grad = dot(branch_block, output_full, 1, 0).astype(BF16)
    attended_grad_t = dot(output_full, branch_block, 0, 1).astype(BF16)
    inner = jnp.sum(
        (attended_grad_t.astype(F32) * result_t).reshape(-1, HEAD_DIM, block), axis=1
    )
    inner = jnp.pad(inner, ((0, 8 - inner.shape[0]), (0, 0)))
    query_grad_t, prompt_grad, own_grad = attend_back(
        meta, queries_t, attended_grad_t, queries, attended_grad, lse, inner, prompt, own
    )
    output_term = dot(branch_block, attended_t, 0, 1).astype(BF16)
    query_term = dot(normed_block, query_grad_t, 0, 1).astype(BF16)
    pair_grad = jnp.concatenate([scatter_prompt(prompt_grad, portion), own_grad], axis=0)
    latent_grad = scatter_features(dot(pair_grad, spread, 1, 1))
    pair_big = dot(latent_all, pair_grad, 0, 0)
    pair_term = jnp.where(mask[:LATENT], pair_big[:LATENT], pair_big[LATENT:]).astype(BF16)
    normed_grad = scatter_true(
        dot(query_grad_t, query_full, 0, 1) + dot(latent_grad, latent_full, 1, 1)
    )
    latent_term = dot(normed_block, latent_grad, 0, 0).astype(BF16)
    pair_terms = pair_term.reshape(columns, pair_rows, strips, 128)
    pair_terms = jnp.concatenate([pair_terms[:, :, i] for i in range(strips)], axis=1)
    pair_terms = pair_terms.reshape(columns * strips * pair_rows, 128)
    early_terms = jnp.concatenate([query_term, latent_term, output_term], axis=1)
    if pair_flat.shape[0] == share:
        early_sums = lax.psum_scatter(
            jnp.concatenate([early_terms, pair_terms], axis=1),
            "col", scatter_dimension=0, tiled=True,
        ).astype(F32)
        pair_sums = early_sums[:, early_terms.shape[1] :]
    else:
        early_sums = lax.psum_scatter(
            early_terms, "col", scatter_dimension=0, tiled=True
        ).astype(F32)
        pair_sums = lax.psum_scatter(
            pair_terms, "col", scatter_dimension=0, tiled=True
        ).astype(F32)
    norm1_grad, first_gain_term = norm_backward(rows, first_scale, first_gain, normed_grad)
    input_gradient = hidden_grad + norm1_grad
    gains = all_sum(jnp.stack([first_gain_term, second_gain_term]))
    pair_sum = jnp.concatenate(
        [pair_sums[i * pair_rows : (i + 1) * pair_rows] for i in range(strips)], axis=1
    )
    return (
        layer,
        input_gradient,
        gains[0],
        early_sums[:, :width],
        early_sums[:, width : width + features],
        pair_sum[:, :width],
        pair_sum[:, width:],
        early_sums[:, width + features : 2 * width + features].T,
        gains[1],
        late_sums[:, :hidden_units],
        late_sums[:, units : units + hidden_units],
        late_sums[:, 2 * units : 2 * units + hidden_units].T,
    )


def solution(mesh):
    rows = P(("col", "row"), None)
    placed = (
        rows, P(), P("col", "row"), P("col", "row"), P("col", "row"), P("col", "row"),
        P("row", "col"), P(), P("col", "row"), P("col", "row"), P("row", "col"), P(), rows,
    )
    given = (
        rows, rows, P(), P("col", "row"), P("col", "row"), P("col", "row"), P("col", "row"),
        P("row", "col"), P(), P("col", "row"), P("col", "row"), P("row", "col"),
    )
    return jax.shard_map(
        per_device, mesh=mesh, in_specs=placed, out_specs=given, check_vma=False
    )
```

```python
import functools

import jax
import jax.numpy as jnp
from jax import lax
from jax.experimental import pallas as pl
from jax.experimental.pallas import tpu as pltpu
from jax.sharding import PartitionSpec as P

HEAD_DIM = 64
LATENT_HEADS = 2
LATENT = 256
PROMPT = 4096
CONT = 512
KEY_TILE = 512
ROW_TILE = 256

epsilon = 1e-05
masked_value = -1e30
BF16 = jnp.bfloat16
F32 = jnp.float32


def dot(left, right, left_dim, right_dim):
    return lax.dot_general(
        left, right, (((left_dim,), (right_dim,)), ((), ())), preferred_element_type=F32
    )


def norm_forward(rows, gain):
    scale = lax.rsqrt(jnp.mean(rows * rows, axis=-1, keepdims=True) + epsilon)
    return (rows * scale * gain, scale)


def norm_backward(rows, scale, gain, grad_out):
    normal = rows * scale
    gain_term = jnp.sum(grad_out * normal, axis=0)
    inner = grad_out * gain
    grad_rows = scale * (inner - normal * jnp.mean(inner * normal, axis=-1, keepdims=True))
    return (grad_rows, gain_term)


def exchange(block, mask):
    return lax.ppermute(block, "row", [(i, i ^ mask) for i in range(lax.axis_size("row"))])


def gather_pieces(rows):
    half = rows.shape[0] // 2
    low, high = rows[:half], rows[half:]
    low_x = exchange(low, 1)
    high_y = exchange(high, 2)
    low_y = exchange(jnp.concatenate([low, low_x], axis=0), 2)
    high_x = exchange(jnp.concatenate([high, high_y], axis=0), 1)
    return [
        (low, high),
        (low_x, high_x[:half]),
        (low_y[:half], high_y),
        (low_y[half:], high_x[half:]),
    ]


def gather_near(rows):
    if lax.axis_size("row") != 4:
        return lax.all_gather(rows, "row", axis=0, tiled=True)
    return jnp.concatenate([part for piece in gather_pieces(rows) for part in piece], axis=0)


def gather_true(rows):
    if lax.axis_size("row") != 4:
        return lax.all_gather(rows, "row", axis=0, tiled=True)
    count = rows.shape[0]
    here = lax.axis_index("row")
    whole = jnp.zeros((4 * count,) + rows.shape[1:], rows.dtype)
    for j, piece in enumerate(gather_pieces(rows)):
        whole = lax.dynamic_update_slice_in_dim(
            whole, jnp.concatenate(piece, axis=0), (here ^ j) * count, 0
        )
    return whole


def scatter_pieces(pieces):
    half = pieces[0].shape[0] // 2
    low = [piece[:half] for piece in pieces]
    high = [piece[half:] for piece in pieces]
    low_in = exchange(jnp.concatenate([low[2], low[3]], axis=0), 2)
    high_in = exchange(jnp.concatenate([high[1], high[3]], axis=0), 1)
    low_on = (low[1].astype(F32) + low_in[half:].astype(F32)).astype(BF16)
    high_on = (high[2].astype(F32) + high_in[half:].astype(F32)).astype(BF16)
    low_last = exchange(low_on, 1)
    high_last = exchange(high_on, 2)
    low_sum = low[0].astype(F32) + low_in[:half].astype(F32) + low_last.astype(F32)
    high_sum = high[0].astype(F32) + high_in[:half].astype(F32) + high_last.astype(F32)
    return jnp.concatenate([low_sum, high_sum], axis=0)


def scatter_near(part):
    part = part.astype(BF16)
    if lax.axis_size("row") != 4:
        return lax.psum_scatter(part, "row", scatter_dimension=0, tiled=True).astype(F32)
    count = part.shape[0] // 4
    return scatter_pieces([part[j * count : (j + 1) * count] for j in range(4)])


def scatter_true(part):
    part = part.astype(BF16)
    if lax.axis_size("row") != 4:
        return lax.psum_scatter(part, "row", scatter_dimension=0, tiled=True).astype(F32)
    count = part.shape[0] // 4
    here = lax.axis_index("row")
    return scatter_pieces(
        [lax.dynamic_slice_in_dim(part, (here ^ j) * count, count, 0) for j in range(4)]
    )


def across(block, mask):
    return lax.ppermute(block, "col", [(i, i ^ mask) for i in range(lax.axis_size("col"))])


def add_low(left, right):
    return (left.astype(F32) + right.astype(F32)).astype(BF16)


def scatter_columns(part):
    part = part.astype(BF16)
    size = lax.axis_size("col")
    if size != 8:
        return lax.psum_scatter(part, "col", scatter_dimension=0, tiled=True).astype(F32)
    count = part.shape[0] // size
    here = lax.axis_index("col")

    def pieces(order):
        return jnp.concatenate(
            [lax.dynamic_slice_in_dim(part, (here ^ j) * count, count, 0) for j in order], axis=0
        )

    mine = pieces((0, 2, 4, 6)).astype(F32) + across(pieces((1, 3, 5, 7)), 1).astype(F32)
    low = mine.astype(BF16)
    got = [across(low[j * count : (j + 1) * count], 2 * j) for j in (1, 2, 3)]
    return (mine[:count] + got[0].astype(F32)) + (got[1].astype(F32) + got[2].astype(F32))


def all_sum(value):
    if lax.axis_size("row") == 4 and lax.axis_size("col") == 8:
        value = (value + exchange(value, 1)) + (exchange(value, 2) + exchange(value, 3))
        value = value + across(value, 1)
        return (value + across(value, 2)) + (across(value, 4) + across(value, 6))
    return lax.psum(value, ("row", "col"))


def masked_heads(tile, heads):
    lanes = lax.broadcasted_iota(jnp.int32, tile.shape, 1) // HEAD_DIM
    return [jnp.where(lanes == h, tile, jnp.zeros_like(tile)) for h in range(heads)]


def one_head(ref, h, rows):
    pair = pl.ds((h // 2) * 2 * HEAD_DIM, 2 * HEAD_DIM)
    own = ref[h * HEAD_DIM : (h + 1) * HEAD_DIM, rows]
    none = jnp.zeros_like(own)
    return pair, jnp.concatenate([own, none] if h % 2 == 0 else [none, own], axis=0)


def visit_tiles(meta, step, prompt_tiles, portion, rows, body):
    place = meta[prompt_tiles + portion // KEY_TILE]
    first_rows = portion // ROW_TILE

    def visit(index, carry):
        is_prompt = index < first_rows
        row0 = index * ROW_TILE
        position = place * portion + row0
        later = row0 - portion
        key0 = step * KEY_TILE
        on_prompt = step < prompt_tiles
        prompt_full = is_prompt & on_prompt & (key0 + KEY_TILE - 1 <= position)
        prompt_part = is_prompt & on_prompt & (key0 <= position + ROW_TILE - 1)
        full = prompt_full | (jnp.logical_not(is_prompt) & on_prompt)
        own_part = (
            jnp.logical_not(is_prompt)
            & jnp.logical_not(on_prompt)
            & (later // CONT == step - prompt_tiles)
        )
        partly = (prompt_part & jnp.logical_not(prompt_full)) | own_part
        ahead = jnp.where(is_prompt, position - key0, later % CONT)

        @pl.when(full)
        def _():
            body(index, None)

        @pl.when(partly)
        def _():
            body(index, ahead)

        return carry

    lax.fori_loop(0, rows // ROW_TILE, visit, 0)


def hide(scores, ahead):
    if ahead is None:
        return scores
    key = lax.broadcasted_iota(jnp.int32, scores.shape, 0)
    query = lax.broadcasted_iota(jnp.int32, scores.shape, 1)
    return jnp.where(key <= query + ahead, scores, masked_value)


def load_pairs(step, near_tiles, meta, near, far, spread, latents):
    place = meta[step]

    @pl.when(place < near_tiles)
    def _():
        latents[...] = near[...]

    @pl.when(place >= near_tiles)
    def _():
        latents[...] = far[...]

    return dot(latents[...], spread[...], 1, 0).astype(BF16)


def attend_kernel(
    meta, q_t, near, far, spread, out, out_low, lse, latents, keys, values_t, acc, top, total,
    *, heads, prompt_tiles, near_tiles, portion, rows,
):
    step = pl.program_id(0)
    width = heads * HEAD_DIM

    @pl.when(step == 0)
    def _():
        acc[...] = jnp.zeros_like(acc)
        top[...] = jnp.full_like(top, masked_value)
        total[...] = jnp.zeros_like(total)

    pairs = load_pairs(step, near_tiles, meta, near, far, spread, latents)
    keys[...] = pairs[:, :width]
    values_t[...] = pairs[:, width:].T

    def body(index, ahead):
        at = pl.ds(pl.multiple_of(index * ROW_TILE, ROW_TILE), ROW_TILE)
        before = top[:, at]
        sums = total[:, at]
        scores = []
        for h in range(heads):
            pair, query = one_head(q_t, h, at)
            scores.append(hide(dot(keys[:, pair], query, 1, 0), ahead))
        nows = []
        news = []
        results = []
        for h in range(heads):
            mine = slice(h * HEAD_DIM, (h + 1) * HEAD_DIM)
            now = jnp.maximum(before[h : h + 1], jnp.max(scores[h], axis=0, keepdims=True))
            probs = jnp.exp(scores[h] - now)
            decay = jnp.exp(before[h : h + 1] - now)
            nows.append(now)
            news.append(decay * sums[h : h + 1] + jnp.sum(probs, axis=0, keepdims=True))
            results.append(
                decay * acc[mine, at] + dot(values_t[mine, :], probs.astype(BF16), 1, 0)
            )
        for h in range(heads):
            top[h : h + 1, at] = nows[h]
            total[h : h + 1, at] = news[h]
            acc[h * HEAD_DIM : (h + 1) * HEAD_DIM, at] = results[h]

    visit_tiles(meta, step, prompt_tiles, portion, rows, body)

    @pl.when(step == pl.num_programs(0) - 1)
    def _():
        lse[...] = top[...] + jnp.log(jnp.maximum(total[...], 1e-37))
        for h in range(heads):
            mine = slice(h * HEAD_DIM, (h + 1) * HEAD_DIM)
            result = acc[mine, :] / total[h : h + 1, :]
            out[mine, :] = result
            out_low[mine, :] = result.astype(BF16)


def attend_back_kernel(
    meta, q_t, grad_t, q, grad, lse, inner, near, far, spread,
    query_grad, latent_grad, pair_grad,
    latents, keys, keys_t, values, queries_apart, grads_apart, query_acc, key_acc, value_acc,
    *, heads, prompt_tiles, near_tiles, portion, rows,
):
    step = pl.program_id(0)
    tall = heads * ROW_TILE
    width = heads * HEAD_DIM

    @pl.when(step == 0)
    def _():
        query_acc[...] = jnp.zeros_like(query_acc)
        pair_grad[...] = jnp.zeros_like(pair_grad)

        def apart(index, carry):
            at = pl.ds(pl.multiple_of(index * ROW_TILE, ROW_TILE), ROW_TILE)
            to = pl.ds(pl.multiple_of(index * tall, tall), tall)
            queries_apart[to, :] = jnp.concatenate(masked_heads(q[at, :], heads), axis=0)
            grads_apart[to, :] = jnp.concatenate(masked_heads(grad[at, :], heads), axis=0)
            return carry

        lax.fori_loop(0, rows // ROW_TILE, apart, 0)

    key_acc[...] = jnp.zeros_like(key_acc)
    value_acc[...] = jnp.zeros_like(value_acc)
    pairs = load_pairs(step, near_tiles, meta, near, far, spread, latents)
    keys[...] = pairs[:, :width]
    keys_t[...] = pairs[:, :width].T
    values[...] = pairs[:, width:]

    def body(index, ahead):
        at = pl.ds(pl.multiple_of(index * ROW_TILE, ROW_TILE), ROW_TILE)
        to = pl.ds(pl.multiple_of(index * tall, tall), tall)
        all_probs = []
        all_grads = []
        for h in range(heads):
            pair, query = one_head(q_t, h, at)
            _, out_grad = one_head(grad_t, h, at)
            scores = hide(dot(keys[:, pair], query, 1, 0), ahead)
            probs = jnp.exp(scores - lse[h : h + 1, at])
            dprobs = dot(values[:, pair], out_grad, 1, 0)
            score_grad = (probs * (dprobs - inner[h : h + 1, at])).astype(BF16)
            mine = slice(h * HEAD_DIM, (h + 1) * HEAD_DIM)
            query_acc[mine, at] += dot(keys_t[mine, :], score_grad, 1, 0)
            all_probs.append(probs.astype(BF16))
            all_grads.append(score_grad)
        value_acc[...] += dot(jnp.concatenate(all_probs, axis=1), grads_apart[to, :], 1, 0)
        key_acc[...] += dot(jnp.concatenate(all_grads, axis=1), queries_apart[to, :], 1, 0)

    visit_tiles(meta, step, prompt_tiles, portion, rows, body)

    pair_low = jnp.concatenate([key_acc[...].astype(BF16), value_acc[...].astype(BF16)], axis=1)
    latent_grad[...] = dot(pair_low, spread[...], 1, 1).astype(BF16)
    pair_grad[...] += dot(latents[...], pair_low, 0, 0)

    @pl.when(step == pl.num_programs(0) - 1)
    def _():
        query_grad[...] = (query_acc[...] * HEAD_DIM**-0.5).astype(BF16)


def whole_spec(shape):
    return pl.BlockSpec(shape, lambda step, meta: (0, 0))


def latent_specs(near, far, spread):
    near_tiles = near.shape[0] // KEY_TILE
    tile = (KEY_TILE, near.shape[1])
    return [
        pl.BlockSpec(tile, lambda step, meta: (jnp.minimum(meta[step], near_tiles - 1), 0)),
        pl.BlockSpec(tile, lambda step, meta: (jnp.maximum(meta[step] - near_tiles, 0), 0)),
        whole_spec(spread.shape),
    ]


def attend(meta, q_t, near, far, spread, portion):
    width, rows = q_t.shape
    heads = width // HEAD_DIM
    prompt_tiles = PROMPT // KEY_TILE
    steps = prompt_tiles + portion // KEY_TILE
    keys = (PROMPT + portion) * rows * heads * 3 // 4
    return pl.pallas_call(
        functools.partial(
            attend_kernel, heads=heads, prompt_tiles=prompt_tiles,
            near_tiles=near.shape[0] // KEY_TILE, portion=portion, rows=rows,
        ),
        grid_spec=pltpu.PrefetchScalarGridSpec(
            num_scalar_prefetch=1,
            grid=(steps,),
            in_specs=[whole_spec((width, rows))] + latent_specs(near, far, spread),
            out_specs=[
                whole_spec((width, rows)),
                whole_spec((width, rows)),
                whole_spec((8, rows)),
            ],
            scratch_shapes=[
                pltpu.VMEM((KEY_TILE, near.shape[1]), BF16),
                pltpu.VMEM((KEY_TILE, width), BF16),
                pltpu.VMEM((width, KEY_TILE), BF16),
                pltpu.VMEM((width, rows), F32),
                pltpu.VMEM((8, rows), F32),
                pltpu.VMEM((8, rows), F32),
            ],
        ),
        out_shape=[
            jax.ShapeDtypeStruct((width, rows), F32),
            jax.ShapeDtypeStruct((width, rows), BF16),
            jax.ShapeDtypeStruct((8, rows), F32),
        ],
        compiler_params=pltpu.CompilerParams(dimension_semantics=("arbitrary",)),
        cost_estimate=pl.CostEstimate(
            flops=keys * HEAD_DIM * 16, transcendentals=keys, bytes_accessed=8 << 20
        ),
        name="attend",
    )(meta, q_t, near, far, spread)


def attend_back(meta, q_t, grad_t, q, grad, lse, inner, near, far, spread, portion):
    width, rows = q_t.shape
    heads = width // HEAD_DIM
    features = near.shape[1]
    prompt_tiles = PROMPT // KEY_TILE
    steps = prompt_tiles + portion // KEY_TILE
    keys = (PROMPT + portion) * rows * heads * 3 // 4
    return pl.pallas_call(
        functools.partial(
            attend_back_kernel, heads=heads, prompt_tiles=prompt_tiles,
            near_tiles=near.shape[0] // KEY_TILE, portion=portion, rows=rows,
        ),
        grid_spec=pltpu.PrefetchScalarGridSpec(
            num_scalar_prefetch=1,
            grid=(steps,),
            in_specs=[
                whole_spec((width, rows)),
                whole_spec((width, rows)),
                whole_spec((rows, width)),
                whole_spec((rows, width)),
                whole_spec((8, rows)),
                whole_spec((8, rows)),
            ]
            + latent_specs(near, far, spread),
            out_specs=[
                whole_spec((width, rows)),
                pl.BlockSpec((KEY_TILE, features), lambda step, meta: (meta[step], 0)),
                whole_spec((features, 2 * width)),
            ],
            scratch_shapes=[
                pltpu.VMEM((KEY_TILE, features), BF16),
                pltpu.VMEM((KEY_TILE, width), BF16),
                pltpu.VMEM((width, KEY_TILE), BF16),
                pltpu.VMEM((KEY_TILE, width), BF16),
                pltpu.VMEM((heads * rows, width), BF16),
                pltpu.VMEM((heads * rows, width), BF16),
                pltpu.VMEM((width, rows), F32),
                pltpu.VMEM((KEY_TILE, width), F32),
                pltpu.VMEM((KEY_TILE, width), F32),
            ],
        ),
        out_shape=[
            jax.ShapeDtypeStruct((width, rows), BF16),
            jax.ShapeDtypeStruct((PROMPT + portion, features), BF16),
            jax.ShapeDtypeStruct((features, 2 * width), F32),
        ],
        compiler_params=pltpu.CompilerParams(dimension_semantics=("arbitrary",)),
        cost_estimate=pl.CostEstimate(
            flops=keys * HEAD_DIM * 40, transcendentals=keys, bytes_accessed=14 << 20
        ),
        name="attend_back",
    )(meta, q_t, grad_t, q, grad, lse, inner, near, far, spread)


def paired_columns(portion):
    return (
        lax.axis_size("row") == 4 and lax.axis_size("col") == 8 and PROMPT // portion == 8
    )


def key_layout(block_order, portion):
    portions = PROMPT // portion
    column = lax.axis_index("col")
    base = column // portions * portions
    ident = block_order[column]
    group = ident // portions
    place = ident % portions
    slots = jnp.arange(block_order.shape[0], dtype=jnp.int32)
    parts = group * portions + jnp.arange(portions, dtype=jnp.int32)
    sources = jnp.sum(jnp.where(block_order[None, :] == parts[:, None], slots[None, :], 0), axis=1)
    split = portion // KEY_TILE
    prompt_tiles = portions * split
    if paired_columns(portion):
        apart = sources ^ column
        tiles = jnp.where(apart % 2 == 0, apart // 2, 5 + apart // 2)
        own = jnp.full((1,), 4, jnp.int32)
    else:
        tiles = (sources - base)[:, None] * split + jnp.arange(split, dtype=jnp.int32)[None, :]
        own = prompt_tiles + jnp.arange(split, dtype=jnp.int32)
    return jnp.concatenate([tiles.reshape(-1), own, place[None]]).astype(jnp.int32)


def bit_of(value, bit):
    return value // (1 << bit) % 2


def swapped(block, axis, distance):
    size = lax.axis_size(axis)
    return lax.ppermute(block, axis, [(i, i ^ 1 << distance) for i in range(size)])


def gather_prompt(held):
    portion = held.shape[0]
    portions = PROMPT // portion
    if portions == lax.axis_size("col"):
        return lax.all_gather(held, "col", axis=0, tiled=True)
    column = lax.axis_index("col")
    for bit in range(portions.bit_length() - 1):
        other = swapped(held, "col", bit)
        upper = bit_of(column, bit) == 1
        held = jnp.where(
            upper, jnp.concatenate([other, held], axis=0), jnp.concatenate([held, other], axis=0)
        )
    return held


def scatter_prompt(buffer, portion):
    portions = PROMPT // portion
    if portions == lax.axis_size("col"):
        return lax.psum_scatter(buffer, "col", scatter_dimension=0, tiled=True)
    column = lax.axis_index("col")
    for bit in reversed(range(portions.bit_length() - 1)):
        half = buffer.shape[0] // 2
        upper = bit_of(column, bit) == 1
        keep = jnp.where(upper, buffer[half:], buffer[:half])
        outgoing = jnp.where(upper, buffer[:half], buffer[half:])
        got = swapped(outgoing, "col", bit)
        buffer = (keep.astype(F32) + got.astype(F32)).astype(BF16)
    return buffer


def gather_latents(part):
    portion = part.shape[0] // 2
    if not paired_columns(portion):
        whole = lax.all_gather(part, "row", axis=1, tiled=True)
        return gather_prompt(whole[:portion]), whole[portion:]
    held = part[:portion]
    held = jnp.concatenate([held, across(held, 2)], axis=0)
    held = jnp.concatenate([held, across(held, 4), part[portion:]], axis=0)
    near = jnp.concatenate(
        [jnp.concatenate(piece, axis=0) for piece in gather_pieces(held)], axis=1
    )
    return near, across(near[: 4 * portion], 1)


def scatter_latents(grad, portion):
    if not paired_columns(portion):
        prompt = scatter_prompt(grad[:PROMPT], portion)
        whole = jnp.concatenate([prompt, grad[PROMPT:]], axis=0)
        return lax.psum_scatter(whole, "row", scatter_dimension=1, tiled=True)
    here = 4 * portion
    near = grad[: here + portion]
    got = across(grad[here + portion :], 1)
    near = jnp.concatenate([add_low(near[:here], got), near[here:]], axis=0)
    width = near.shape[1] // 4
    mine = scatter_pieces([near[:, j * width : (j + 1) * width] for j in range(4)])
    low = mine[:here].astype(BF16)
    blocks = [low[j * portion : (j + 1) * portion] for j in range(4)]
    got = across(jnp.concatenate([blocks[1], blocks[3]], axis=0), 2)
    other = across(add_low(blocks[2], got[portion:]), 4)
    prompt = mine[:portion] + got[:portion].astype(F32) + other.astype(F32)
    return jnp.concatenate([prompt.astype(BF16), mine[here:].astype(BF16)], axis=0)


def near_features(table, portion):
    if not paired_columns(portion):
        return table
    here = lax.axis_index("row")
    count = table.shape[0] // 4
    return jnp.concatenate(
        [lax.dynamic_slice_in_dim(table, (here ^ j) * count, count, 0) for j in range(4)], axis=0
    )


def padded(block, width):
    return jnp.pad(block, ((0, 0), (0, width - block.shape[1])))


def head_mask(width):
    group = lax.broadcasted_iota(jnp.int32, (LATENT_HEADS * LATENT, 2 * width), 0) // LATENT
    head = lax.broadcasted_iota(jnp.int32, (LATENT_HEADS * LATENT, 2 * width), 1) // HEAD_DIM
    return group == head % LATENT_HEADS


def per_device(
    tokens, first_gain, query_weight, latent_weight, key_weight, value_weight, output_weight,
    second_gain, gate_weight, up_weight, down_weight, block_order, cotangent,
):
    columns = lax.axis_size("col")
    share = query_weight.shape[0]
    width = query_weight.shape[1]
    features = latent_weight.shape[1]
    hidden_units = gate_weight.shape[1]
    units = -(-hidden_units // 128) * 128

    early = jnp.concatenate(
        [query_weight, latent_weight, output_weight.T], axis=1
    )
    pair_weight = jnp.concatenate([key_weight, value_weight], axis=1)
    late = jnp.concatenate(
        [padded(gate_weight, units), padded(up_weight, units), padded(down_weight.T, units)], axis=1
    )
    pair_rows = pair_weight.shape[0]
    strips = 2 * width // 128
    pair_flat = jnp.concatenate(
        [pair_weight[:, i * 128 : (i + 1) * 128] for i in range(strips)], axis=0
    )
    if pair_flat.shape[0] == share:
        early_all = lax.all_gather(
            jnp.concatenate([early, pair_flat], axis=1), "col", axis=0, tiled=True
        )
        flat_all = early_all[:, early.shape[1] :].reshape(columns, strips, pair_rows, 128)
    else:
        early_all = lax.all_gather(early, "col", axis=0, tiled=True)
        flat_all = lax.all_gather(pair_flat, "col", axis=0, tiled=True).reshape(
            columns, strips, pair_rows, 128
        )
    pair_full = jnp.concatenate(
        [flat_all[:, i].reshape(columns * pair_rows, 128) for i in range(strips)], axis=1
    )
    query_full = early_all[:, :width]
    latent_full = early_all[:, width : width + features]
    output_full = early_all[:, width + features : 2 * width + features]

    rows = tokens.astype(F32)
    normed, first_scale = norm_forward(rows, first_gain)
    normed_block = gather_true(normed.astype(BF16))
    block = normed_block.shape[0]
    portion = block // 2
    mask = head_mask(width)
    spread = jnp.where(mask, jnp.concatenate([pair_full] * LATENT_HEADS, axis=0), jnp.zeros((), BF16))
    spread = near_features(spread, portion)
    latent_part = dot(normed_block, latent_full, 1, 0).astype(BF16)
    cotangent_later, latent_part = lax.optimization_barrier((cotangent, latent_part))
    cot_block = gather_near(cotangent_later)
    near, far = gather_latents(latent_part)
    scale = HEAD_DIM**-0.5
    queries_t = (dot(query_full, normed_block, 0, 1).astype(BF16) * scale).astype(BF16)
    queries = (dot(normed_block, query_full, 1, 0).astype(BF16) * scale).astype(BF16)
    meta = key_layout(block_order, portion)
    late, near, far, cot_block = lax.optimization_barrier((late, near, far, cot_block))
    late_all = lax.all_gather(late, "col", axis=0, tiled=True)
    wide_full = late_all[:, : 2 * units]
    down_full = late_all[:, 2 * units :]
    result_t, attended_t, lse = attend(meta, queries_t, near, far, spread, portion)
    branch = dot(attended_t, output_full, 0, 1)
    hidden = rows + scatter_true(branch)

    normed2, second_scale = norm_forward(hidden, second_gain)
    normed2_block = gather_near(normed2.astype(BF16))
    both = dot(normed2_block, wide_full, 1, 0)
    gate = both[:, :units]
    up = both[:, units:]
    sigma = jax.nn.sigmoid(gate)
    act = (gate * sigma * up).astype(BF16)
    act_grad = dot(cot_block, down_full, 1, 0)
    gate_grad = (act_grad * up * sigma * (1.0 + gate * (1.0 - sigma))).astype(BF16)
    up_grad = (act_grad * gate * sigma).astype(BF16)
    both_grad = jnp.concatenate([gate_grad, up_grad], axis=1)
    normed2_grad = scatter_near(dot(both_grad, wide_full, 1, 1))
    late_terms = jnp.concatenate(
        [
            dot(normed2_block, both_grad, 0, 0).astype(BF16),
            dot(cot_block, act, 0, 0).astype(BF16),
        ],
        axis=1,
    )
    late_sums = lax.psum_scatter(late_terms, "col", scatter_dimension=0, tiled=True).astype(F32)
    norm2_grad, second_gain_term = norm_backward(hidden, second_scale, second_gain, normed2_grad)
    hidden_grad = cotangent.astype(F32) + norm2_grad

    branch_block = gather_true(hidden_grad.astype(BF16))
    act, branch_block = lax.optimization_barrier((act, branch_block))
    layer = hidden + scatter_near(dot(act, down_full, 1, 1))
    attended_grad = dot(branch_block, output_full, 1, 0).astype(BF16)
    attended_grad_t = dot(output_full, branch_block, 0, 1).astype(BF16)
    inner = jnp.sum(
        (attended_grad_t.astype(F32) * result_t).reshape(-1, HEAD_DIM, block), axis=1
    )
    inner = jnp.pad(inner, ((0, 8 - inner.shape[0]), (0, 0)))
    query_grad_t, latent_terms, pair_big = attend_back(
        meta, queries_t, attended_grad_t, queries, attended_grad, lse, inner, near, far, spread,
        portion,
    )
    latent_grad = scatter_latents(latent_terms, portion)
    output_term = dot(branch_block, attended_t, 0, 1).astype(BF16)
    query_term = dot(normed_block, query_grad_t, 0, 1).astype(BF16)
    pair_big = near_features(pair_big, portion)
    pair_term = jnp.where(mask[:LATENT], pair_big[:LATENT], pair_big[LATENT:]).astype(BF16)
    pair_terms = pair_term.reshape(columns, pair_rows, strips, 128)
    pair_terms = jnp.concatenate([pair_terms[:, :, i] for i in range(strips)], axis=1)
    pair_terms = pair_terms.reshape(columns * strips * pair_rows, 128)
    early_terms = jnp.concatenate([query_term, output_term], axis=1)
    if pair_flat.shape[0] == share:
        early_sums = lax.psum_scatter(
            jnp.concatenate([early_terms, pair_terms], axis=1),
            "col", scatter_dimension=0, tiled=True,
        ).astype(F32)
        pair_sums = early_sums[:, early_terms.shape[1] :]
    else:
        early_sums = lax.psum_scatter(
            early_terms, "col", scatter_dimension=0, tiled=True
        ).astype(F32)
        pair_sums = lax.psum_scatter(
            pair_terms, "col", scatter_dimension=0, tiled=True
        ).astype(F32)
    latent_sums = scatter_columns(dot(normed_block, latent_grad, 0, 0))
    normed_grad = scatter_true(
        dot(query_grad_t, query_full, 0, 1) + dot(latent_grad, latent_full, 1, 1)
    )
    norm1_grad, first_gain_term = norm_backward(rows, first_scale, first_gain, normed_grad)
    input_gradient = hidden_grad + norm1_grad
    gains = all_sum(jnp.stack([first_gain_term, second_gain_term]))
    pair_sum = jnp.concatenate(
        [pair_sums[i * pair_rows : (i + 1) * pair_rows] for i in range(strips)], axis=1
    )
    return (
        layer,
        input_gradient,
        gains[0],
        early_sums[:, :width],
        latent_sums,
        pair_sum[:, :width],
        pair_sum[:, width:],
        early_sums[:, width : 2 * width].T,
        gains[1],
        late_sums[:, :hidden_units],
        late_sums[:, units : units + hidden_units],
        late_sums[:, 2 * units : 2 * units + hidden_units].T,
    )


def solution(mesh):
    rows = P(("col", "row"), None)
    placed = (
        rows, P(), P("col", "row"), P("col", "row"), P("col", "row"), P("col", "row"),
        P("row", "col"), P(), P("col", "row"), P("col", "row"), P("row", "col"), P(), rows,
    )
    given = (
        rows, rows, P(), P("col", "row"), P("col", "row"), P("col", "row"), P("col", "row"),
        P("row", "col"), P(), P("col", "row"), P("col", "row"), P("row", "col"),
    )
    return jax.shard_map(
        per_device, mesh=mesh, in_specs=placed, out_specs=given, check_vma=False
    )
```

```python
import functools

import jax
import jax.numpy as jnp
from jax import lax
from jax.experimental import pallas as pl
from jax.experimental.pallas import tpu as pltpu
from jax.sharding import PartitionSpec as P

HEAD_DIM = 64
LATENT_HEADS = 2
LATENT = 256
PROMPT = 4096
CONT = 512
KEY_TILE = 512
ROW_TILE = 256

epsilon = 1e-05
masked_value = -1e30
BF16 = jnp.bfloat16
F32 = jnp.float32


def dot(left, right, left_dim, right_dim):
    return lax.dot_general(
        left, right, (((left_dim,), (right_dim,)), ((), ())), preferred_element_type=F32
    )


def norm_forward(rows, gain):
    scale = lax.rsqrt(jnp.mean(rows * rows, axis=-1, keepdims=True) + epsilon)
    return (rows * scale * gain, scale)


def norm_backward(rows, scale, gain, grad_out):
    normal = rows * scale
    gain_term = jnp.sum(grad_out * normal, axis=0)
    inner = grad_out * gain
    grad_rows = scale * (inner - normal * jnp.mean(inner * normal, axis=-1, keepdims=True))
    return (grad_rows, gain_term)


def exchange(block, mask):
    return lax.ppermute(block, "row", [(i, i ^ mask) for i in range(lax.axis_size("row"))])


def together(*values):
    return lax.optimization_barrier(values)


def gather_first(rows):
    half = rows.shape[0] // 2
    return exchange(rows[:half], 1), exchange(rows[half:], 2)


def gather_second(rows, low_x, high_y):
    half = rows.shape[0] // 2
    low_y = exchange(jnp.concatenate([rows[:half], low_x], axis=0), 2)
    high_x = exchange(jnp.concatenate([rows[half:], high_y], axis=0), 1)
    return low_y, high_x


def gather_order(rows, low_x, high_y, low_y, high_x):
    half = rows.shape[0] // 2
    return [
        (rows[:half], rows[half:]),
        (low_x, high_x[:half]),
        (low_y[:half], high_y),
        (low_y[half:], high_x[half:]),
    ]


def gather_pieces(rows):
    first = together(*gather_first(rows))
    return gather_order(rows, *first, *together(*gather_second(rows, *first)))


def join(pieces):
    return jnp.concatenate([part for piece in pieces for part in piece], axis=0)


def gather_near(rows):
    if lax.axis_size("row") != 4:
        return lax.all_gather(rows, "row", axis=0, tiled=True)
    return join(gather_pieces(rows))


def gather_true(rows):
    if lax.axis_size("row") != 4:
        return lax.all_gather(rows, "row", axis=0, tiled=True)
    count = rows.shape[0]
    here = lax.axis_index("row")
    whole = jnp.zeros((4 * count,) + rows.shape[1:], rows.dtype)
    for j, piece in enumerate(gather_pieces(rows)):
        whole = lax.dynamic_update_slice_in_dim(
            whole, jnp.concatenate(piece, axis=0), (here ^ j) * count, 0
        )
    return whole


def scatter_first(pieces):
    half = pieces[0].shape[0] // 2
    return (
        exchange(jnp.concatenate([pieces[2][:half], pieces[3][:half]], axis=0), 2),
        exchange(jnp.concatenate([pieces[1][half:], pieces[3][half:]], axis=0), 1),
    )


def scatter_second(pieces, low_in, high_in):
    half = pieces[0].shape[0] // 2
    return (
        exchange(add_low(pieces[1][:half], low_in[half:]), 1),
        exchange(add_low(pieces[2][half:], high_in[half:]), 2),
    )


def scatter_last(pieces, low_in, high_in, low_last, high_last):
    half = pieces[0].shape[0] // 2
    low = pieces[0][:half].astype(F32) + low_in[:half].astype(F32) + low_last.astype(F32)
    high = pieces[0][half:].astype(F32) + high_in[:half].astype(F32) + high_last.astype(F32)
    return jnp.concatenate([low, high], axis=0)


def scatter_pieces(pieces):
    first = together(*scatter_first(pieces))
    return scatter_last(pieces, *first, *together(*scatter_second(pieces, *first)))


def add_low(left, right):
    return (left.astype(F32) + right.astype(F32)).astype(BF16)


def scatter_near(part):
    part = part.astype(BF16)
    if lax.axis_size("row") != 4:
        return lax.psum_scatter(part, "row", scatter_dimension=0, tiled=True).astype(F32)
    count = part.shape[0] // 4
    return scatter_pieces([part[j * count : (j + 1) * count] for j in range(4)])


def true_pieces(part):
    count = part.shape[0] // 4
    here = lax.axis_index("row")
    return [lax.dynamic_slice_in_dim(part, (here ^ j) * count, count, 0) for j in range(4)]


def scatter_true(part):
    part = part.astype(BF16)
    if lax.axis_size("row") != 4:
        return lax.psum_scatter(part, "row", scatter_dimension=0, tiled=True).astype(F32)
    return scatter_pieces(true_pieces(part))


def across(block, mask):
    return lax.ppermute(block, "col", [(i, i ^ mask) for i in range(lax.axis_size("col"))])


def column_first(part):
    size = lax.axis_size("col")
    count = part.shape[0] // size
    here = lax.axis_index("col")

    def pieces(order):
        return jnp.concatenate(
            [lax.dynamic_slice_in_dim(part, (here ^ j) * count, count, 0) for j in order], axis=0
        )

    return pieces((0, 2, 4, 6)), across(pieces((1, 3, 5, 7)), 1)


def column_second(mine, got):
    count = mine.shape[0] // 4
    mine = mine.astype(F32) + got.astype(F32)
    low = mine.astype(BF16)
    return mine[:count], [across(low[j * count : (j + 1) * count], 2 * j) for j in (1, 2, 3)]


def column_last(mine, got):
    return (mine + got[0].astype(F32)) + (got[1].astype(F32) + got[2].astype(F32))


def all_sum(value):
    if lax.axis_size("row") == 4 and lax.axis_size("col") == 8:
        value = (value + exchange(value, 1)) + (exchange(value, 2) + exchange(value, 3))
        value = value + across(value, 1)
        return (value + across(value, 2)) + (across(value, 4) + across(value, 6))
    return lax.psum(value, ("row", "col"))


def masked_heads(tile, heads):
    lanes = lax.broadcasted_iota(jnp.int32, tile.shape, 1) // HEAD_DIM
    return [jnp.where(lanes == h, tile, jnp.zeros_like(tile)) for h in range(heads)]


def one_head(ref, h, rows):
    pair = pl.ds((h // 2) * 2 * HEAD_DIM, 2 * HEAD_DIM)
    own = ref[h * HEAD_DIM : (h + 1) * HEAD_DIM, rows]
    none = jnp.zeros_like(own)
    return pair, jnp.concatenate([own, none] if h % 2 == 0 else [none, own], axis=0)


def visit_tiles(meta, step, prompt_tiles, portion, rows, body):
    place = meta[prompt_tiles + portion // KEY_TILE]
    first_rows = portion // ROW_TILE

    def visit(index, carry):
        is_prompt = index < first_rows
        row0 = index * ROW_TILE
        position = place * portion + row0
        later = row0 - portion
        key0 = step * KEY_TILE
        on_prompt = step < prompt_tiles
        prompt_full = is_prompt & on_prompt & (key0 + KEY_TILE - 1 <= position)
        prompt_part = is_prompt & on_prompt & (key0 <= position + ROW_TILE - 1)
        full = prompt_full | (jnp.logical_not(is_prompt) & on_prompt)
        own_part = (
            jnp.logical_not(is_prompt)
            & jnp.logical_not(on_prompt)
            & (later // CONT == step - prompt_tiles)
        )
        partly = (prompt_part & jnp.logical_not(prompt_full)) | own_part
        ahead = jnp.where(is_prompt, position - key0, later % CONT)

        @pl.when(full)
        def _():
            body(index, None)

        @pl.when(partly)
        def _():
            body(index, ahead)

        return carry

    lax.fori_loop(0, rows // ROW_TILE, visit, 0)


def hide(scores, ahead):
    if ahead is None:
        return scores
    key = lax.broadcasted_iota(jnp.int32, scores.shape, 0)
    query = lax.broadcasted_iota(jnp.int32, scores.shape, 1)
    return jnp.where(key <= query + ahead, scores, masked_value)


def load_pairs(step, near_tiles, meta, near, far, spread, latents):
    place = meta[step]

    @pl.when(place < near_tiles)
    def _():
        latents[...] = jnp.concatenate([near[j] for j in range(near.shape[0])], axis=1)

    @pl.when(place >= near_tiles)
    def _():
        latents[...] = jnp.concatenate([far[j] for j in range(far.shape[0])], axis=1)

    return dot(latents[...], spread[...], 1, 0).astype(BF16)


def attend_kernel(
    meta, q_t, near, far, spread, out, out_low, lse, latents, keys, values_t, acc, top, total,
    *, heads, prompt_tiles, near_tiles, portion, rows,
):
    step = pl.program_id(0)
    width = heads * HEAD_DIM

    @pl.when(step == 0)
    def _():
        acc[...] = jnp.zeros_like(acc)
        top[...] = jnp.full_like(top, masked_value)
        total[...] = jnp.zeros_like(total)

    pairs = load_pairs(step, near_tiles, meta, near, far, spread, latents)
    keys[...] = pairs[:, :width]
    values_t[...] = pairs[:, width:].T

    def body(index, ahead):
        at = pl.ds(pl.multiple_of(index * ROW_TILE, ROW_TILE), ROW_TILE)
        before = top[:, at]
        sums = total[:, at]
        scores = []
        for h in range(heads):
            pair, query = one_head(q_t, h, at)
            scores.append(hide(dot(keys[:, pair], query, 1, 0), ahead))
        nows = []
        news = []
        results = []
        for h in range(heads):
            mine = slice(h * HEAD_DIM, (h + 1) * HEAD_DIM)
            now = jnp.maximum(before[h : h + 1], jnp.max(scores[h], axis=0, keepdims=True))
            probs = jnp.exp(scores[h] - now)
            decay = jnp.exp(before[h : h + 1] - now)
            nows.append(now)
            news.append(decay * sums[h : h + 1] + jnp.sum(probs, axis=0, keepdims=True))
            results.append(
                decay * acc[mine, at] + dot(values_t[mine, :], probs.astype(BF16), 1, 0)
            )
        for h in range(heads):
            top[h : h + 1, at] = nows[h]
            total[h : h + 1, at] = news[h]
            acc[h * HEAD_DIM : (h + 1) * HEAD_DIM, at] = results[h]

    visit_tiles(meta, step, prompt_tiles, portion, rows, body)

    @pl.when(step == pl.num_programs(0) - 1)
    def _():
        lse[...] = top[...] + jnp.log(jnp.maximum(total[...], 1e-37))
        for h in range(heads):
            mine = slice(h * HEAD_DIM, (h + 1) * HEAD_DIM)
            result = acc[mine, :] / total[h : h + 1, :]
            out[mine, :] = result
            out_low[mine, :] = result.astype(BF16)


def attend_back_kernel(
    meta, q_t, grad_t, q, grad, lse, inner, near, far, spread,
    query_grad, latent_grad, pair_grad,
    latents, keys, keys_t, values, queries_apart, grads_apart, query_acc, key_acc, value_acc,
    *, heads, prompt_tiles, near_tiles, portion, rows,
):
    step = pl.program_id(0)
    tall = heads * ROW_TILE
    width = heads * HEAD_DIM

    @pl.when(step == 0)
    def _():
        query_acc[...] = jnp.zeros_like(query_acc)
        pair_grad[...] = jnp.zeros_like(pair_grad)

        def apart(index, carry):
            at = pl.ds(pl.multiple_of(index * ROW_TILE, ROW_TILE), ROW_TILE)
            to = pl.ds(pl.multiple_of(index * tall, tall), tall)
            queries_apart[to, :] = jnp.concatenate(masked_heads(q[at, :], heads), axis=0)
            grads_apart[to, :] = jnp.concatenate(masked_heads(grad[at, :], heads), axis=0)
            return carry

        lax.fori_loop(0, rows // ROW_TILE, apart, 0)

    key_acc[...] = jnp.zeros_like(key_acc)
    value_acc[...] = jnp.zeros_like(value_acc)
    pairs = load_pairs(step, near_tiles, meta, near, far, spread, latents)
    keys[...] = pairs[:, :width]
    keys_t[...] = pairs[:, :width].T
    values[...] = pairs[:, width:]

    def body(index, ahead):
        at = pl.ds(pl.multiple_of(index * ROW_TILE, ROW_TILE), ROW_TILE)
        to = pl.ds(pl.multiple_of(index * tall, tall), tall)
        all_probs = []
        all_grads = []
        for h in range(heads):
            pair, query = one_head(q_t, h, at)
            _, out_grad = one_head(grad_t, h, at)
            scores = hide(dot(keys[:, pair], query, 1, 0), ahead)
            probs = jnp.exp(scores - lse[h : h + 1, at])
            dprobs = dot(values[:, pair], out_grad, 1, 0)
            score_grad = (probs * (dprobs - inner[h : h + 1, at])).astype(BF16)
            mine = slice(h * HEAD_DIM, (h + 1) * HEAD_DIM)
            query_acc[mine, at] += dot(keys_t[mine, :], score_grad, 1, 0)
            all_probs.append(probs.astype(BF16))
            all_grads.append(score_grad)
        value_acc[...] += dot(jnp.concatenate(all_probs, axis=1), grads_apart[to, :], 1, 0)
        key_acc[...] += dot(jnp.concatenate(all_grads, axis=1), queries_apart[to, :], 1, 0)

    visit_tiles(meta, step, prompt_tiles, portion, rows, body)

    pair_low = jnp.concatenate([key_acc[...].astype(BF16), value_acc[...].astype(BF16)], axis=1)
    grads = dot(pair_low, spread[...], 1, 1).astype(BF16)
    for j in range(latent_grad.shape[0]):
        latent_grad[j] = grads[:, j * 128 : (j + 1) * 128]
    pair_grad[...] += dot(latents[...], pair_low, 0, 0)

    @pl.when(step == pl.num_programs(0) - 1)
    def _():
        query_grad[...] = (query_acc[...] * HEAD_DIM**-0.5).astype(BF16)


def whole_spec(shape):
    return pl.BlockSpec(shape, lambda step, meta: (0, 0))


def latent_specs(near, far, spread):
    near_tiles = near.shape[1] // KEY_TILE
    tile = (near.shape[0], KEY_TILE, 128)
    return [
        pl.BlockSpec(tile, lambda step, meta: (0, jnp.minimum(meta[step], near_tiles - 1), 0)),
        pl.BlockSpec(tile, lambda step, meta: (0, jnp.maximum(meta[step] - near_tiles, 0), 0)),
        whole_spec(spread.shape),
    ]


def attend(meta, q_t, near, far, spread, portion):
    width, rows = q_t.shape
    heads = width // HEAD_DIM
    prompt_tiles = PROMPT // KEY_TILE
    steps = prompt_tiles + portion // KEY_TILE
    keys = (PROMPT + portion) * rows * heads * 3 // 4
    return pl.pallas_call(
        functools.partial(
            attend_kernel, heads=heads, prompt_tiles=prompt_tiles,
            near_tiles=near.shape[1] // KEY_TILE, portion=portion, rows=rows,
        ),
        grid_spec=pltpu.PrefetchScalarGridSpec(
            num_scalar_prefetch=1,
            grid=(steps,),
            in_specs=[whole_spec((width, rows))] + latent_specs(near, far, spread),
            out_specs=[
                whole_spec((width, rows)),
                whole_spec((width, rows)),
                whole_spec((8, rows)),
            ],
            scratch_shapes=[
                pltpu.VMEM((KEY_TILE, spread.shape[0]), BF16),
                pltpu.VMEM((KEY_TILE, width), BF16),
                pltpu.VMEM((width, KEY_TILE), BF16),
                pltpu.VMEM((width, rows), F32),
                pltpu.VMEM((8, rows), F32),
                pltpu.VMEM((8, rows), F32),
            ],
        ),
        out_shape=[
            jax.ShapeDtypeStruct((width, rows), F32),
            jax.ShapeDtypeStruct((width, rows), BF16),
            jax.ShapeDtypeStruct((8, rows), F32),
        ],
        compiler_params=pltpu.CompilerParams(dimension_semantics=("arbitrary",)),
        cost_estimate=pl.CostEstimate(
            flops=keys * HEAD_DIM * 16, transcendentals=keys, bytes_accessed=8 << 20
        ),
        name="attend",
    )(meta, q_t, near, far, spread)


def attend_back(meta, q_t, grad_t, q, grad, lse, inner, near, far, spread, portion):
    width, rows = q_t.shape
    heads = width // HEAD_DIM
    planes = near.shape[0]
    features = spread.shape[0]
    prompt_tiles = PROMPT // KEY_TILE
    steps = prompt_tiles + portion // KEY_TILE
    keys = (PROMPT + portion) * rows * heads * 3 // 4
    return pl.pallas_call(
        functools.partial(
            attend_back_kernel, heads=heads, prompt_tiles=prompt_tiles,
            near_tiles=near.shape[1] // KEY_TILE, portion=portion, rows=rows,
        ),
        grid_spec=pltpu.PrefetchScalarGridSpec(
            num_scalar_prefetch=1,
            grid=(steps,),
            in_specs=[
                whole_spec((width, rows)),
                whole_spec((width, rows)),
                whole_spec((rows, width)),
                whole_spec((rows, width)),
                whole_spec((8, rows)),
                whole_spec((8, rows)),
            ]
            + latent_specs(near, far, spread),
            out_specs=[
                whole_spec((width, rows)),
                pl.BlockSpec((planes, KEY_TILE, 128), lambda step, meta: (0, meta[step], 0)),
                whole_spec((features, 2 * width)),
            ],
            scratch_shapes=[
                pltpu.VMEM((KEY_TILE, features), BF16),
                pltpu.VMEM((KEY_TILE, width), BF16),
                pltpu.VMEM((width, KEY_TILE), BF16),
                pltpu.VMEM((KEY_TILE, width), BF16),
                pltpu.VMEM((heads * rows, width), BF16),
                pltpu.VMEM((heads * rows, width), BF16),
                pltpu.VMEM((width, rows), F32),
                pltpu.VMEM((KEY_TILE, width), F32),
                pltpu.VMEM((KEY_TILE, width), F32),
            ],
        ),
        out_shape=[
            jax.ShapeDtypeStruct((width, rows), BF16),
            jax.ShapeDtypeStruct((planes, PROMPT + portion, 128), BF16),
            jax.ShapeDtypeStruct((features, 2 * width), F32),
        ],
        compiler_params=pltpu.CompilerParams(dimension_semantics=("arbitrary",)),
        cost_estimate=pl.CostEstimate(
            flops=keys * HEAD_DIM * 40, transcendentals=keys, bytes_accessed=14 << 20
        ),
        name="attend_back",
    )(meta, q_t, grad_t, q, grad, lse, inner, near, far, spread)


def paired_columns(portion):
    return (
        lax.axis_size("row") == 4 and lax.axis_size("col") == 8 and PROMPT // portion == 8
    )


def key_layout(block_order, portion):
    portions = PROMPT // portion
    column = lax.axis_index("col")
    base = column // portions * portions
    ident = block_order[column]
    group = ident // portions
    place = ident % portions
    slots = jnp.arange(block_order.shape[0], dtype=jnp.int32)
    parts = group * portions + jnp.arange(portions, dtype=jnp.int32)
    sources = jnp.sum(jnp.where(block_order[None, :] == parts[:, None], slots[None, :], 0), axis=1)
    split = portion // KEY_TILE
    prompt_tiles = portions * split
    if paired_columns(portion):
        apart = sources ^ column
        tiles = jnp.where(apart % 2 == 0, apart // 2, 5 + apart // 2)
        own = jnp.full((1,), 4, jnp.int32)
    else:
        tiles = (sources - base)[:, None] * split + jnp.arange(split, dtype=jnp.int32)[None, :]
        own = prompt_tiles + jnp.arange(split, dtype=jnp.int32)
    return jnp.concatenate([tiles.reshape(-1), own, place[None]]).astype(jnp.int32)


def bit_of(value, bit):
    return value // (1 << bit) % 2


def swapped(block, axis, distance):
    size = lax.axis_size(axis)
    return lax.ppermute(block, axis, [(i, i ^ 1 << distance) for i in range(size)])


def gather_prompt(held):
    portion = held.shape[0]
    portions = PROMPT // portion
    if portions == lax.axis_size("col"):
        return lax.all_gather(held, "col", axis=0, tiled=True)
    column = lax.axis_index("col")
    for bit in range(portions.bit_length() - 1):
        other = swapped(held, "col", bit)
        upper = bit_of(column, bit) == 1
        held = jnp.where(
            upper, jnp.concatenate([other, held], axis=0), jnp.concatenate([held, other], axis=0)
        )
    return held


def scatter_prompt(buffer, portion):
    portions = PROMPT // portion
    if portions == lax.axis_size("col"):
        return lax.psum_scatter(buffer, "col", scatter_dimension=0, tiled=True)
    column = lax.axis_index("col")
    for bit in reversed(range(portions.bit_length() - 1)):
        half = buffer.shape[0] // 2
        upper = bit_of(column, bit) == 1
        keep = jnp.where(upper, buffer[half:], buffer[:half])
        outgoing = jnp.where(upper, buffer[:half], buffer[half:])
        got = swapped(outgoing, "col", bit)
        buffer = (keep.astype(F32) + got.astype(F32)).astype(BF16)
    return buffer


def planes_of(whole):
    return jnp.stack([whole[:, j : j + 128] for j in range(0, whole.shape[1], 128)], axis=0)


def gather_latents(part, beside):
    portion = part.shape[0] // 2
    if not paired_columns(portion):
        whole = lax.all_gather(part, "row", axis=1, tiled=True)
        near = planes_of(gather_prompt(whole[:portion]))
        return near, planes_of(whole[portion:]), near[:, :8], gather_near(beside)
    held = part[:portion]
    beside, held = together(beside, held)
    got, *first = together(across(held, 2), *gather_first(beside))
    held = jnp.concatenate([held, got], axis=0)
    got, *second = together(across(held, 4), *gather_second(beside, *first))
    beside = join(gather_order(beside, *first, *second))
    held = jnp.concatenate([held, got, part[portion:]], axis=0)
    near = jnp.stack([jnp.concatenate(piece, axis=0) for piece in gather_pieces(held)], axis=0)
    return near, across(near[:, : 4 * portion], 1), got, beside


def scatter_latents(grad, portion, column_terms):
    if not paired_columns(portion):
        whole = jnp.concatenate([grad[j] for j in range(grad.shape[0])], axis=1)
        prompt = scatter_prompt(whole[:PROMPT], portion)
        whole = jnp.concatenate([prompt, whole[PROMPT:]], axis=0)
        sums = lax.psum_scatter(
            column_terms(), "col", scatter_dimension=0, tiled=True
        ).astype(F32)
        return lax.psum_scatter(whole, "row", scatter_dimension=1, tiled=True), sums
    here = 4 * portion
    got = across(grad[:, here + portion :], 1)
    pieces = [
        jnp.concatenate(
            [add_low(grad[j, :here], got[j]), grad[j, here : here + portion]], axis=0
        )
        for j in range(4)
    ]
    terms, terms_got = column_first(column_terms())
    terms_got, *first = together(terms_got, *scatter_first(pieces))
    terms, terms_on = column_second(terms, terms_got)
    *terms_on, low_last, high_last = together(*terms_on, *scatter_second(pieces, *first))
    mine = scatter_last(pieces, *first, low_last, high_last)
    low = mine[:here].astype(BF16)
    blocks = [low[j * portion : (j + 1) * portion] for j in range(4)]
    got = across(jnp.concatenate([blocks[1], blocks[3]], axis=0), 2)
    other = across(add_low(blocks[2], got[portion:]), 4)
    prompt = mine[:portion] + got[:portion].astype(F32) + other.astype(F32)
    sums = column_last(terms, terms_on)
    return jnp.concatenate([prompt.astype(BF16), mine[here:].astype(BF16)], axis=0), sums


def near_features(table, portion):
    if not paired_columns(portion):
        return table
    here = lax.axis_index("row")
    count = table.shape[0] // 4
    return jnp.concatenate(
        [lax.dynamic_slice_in_dim(table, (here ^ j) * count, count, 0) for j in range(4)], axis=0
    )


def padded(block, width):
    return jnp.pad(block, ((0, 0), (0, width - block.shape[1])))


def head_mask(width):
    group = lax.broadcasted_iota(jnp.int32, (LATENT_HEADS * LATENT, 2 * width), 0) // LATENT
    head = lax.broadcasted_iota(jnp.int32, (LATENT_HEADS * LATENT, 2 * width), 1) // HEAD_DIM
    return group == head % LATENT_HEADS


def per_device(
    tokens, first_gain, query_weight, latent_weight, key_weight, value_weight, output_weight,
    second_gain, gate_weight, up_weight, down_weight, block_order, cotangent,
):
    columns = lax.axis_size("col")
    share = query_weight.shape[0]
    width = query_weight.shape[1]
    features = latent_weight.shape[1]
    hidden_units = gate_weight.shape[1]
    units = -(-hidden_units // 128) * 128

    early = jnp.concatenate(
        [query_weight, latent_weight, output_weight.T], axis=1
    )
    pair_weight = jnp.concatenate([key_weight, value_weight], axis=1)
    late = jnp.concatenate(
        [padded(gate_weight, units), padded(up_weight, units), padded(down_weight.T, units)], axis=1
    )
    pair_rows = pair_weight.shape[0]
    strips = 2 * width // 128
    pair_flat = jnp.concatenate(
        [pair_weight[:, i * 128 : (i + 1) * 128] for i in range(strips)], axis=0
    )
    if pair_flat.shape[0] == share:
        early_all = lax.all_gather(
            jnp.concatenate([early, pair_flat], axis=1), "col", axis=0, tiled=True
        )
        flat_all = early_all[:, early.shape[1] :].reshape(columns, strips, pair_rows, 128)
    else:
        early_all = lax.all_gather(early, "col", axis=0, tiled=True)
        flat_all = lax.all_gather(pair_flat, "col", axis=0, tiled=True).reshape(
            columns, strips, pair_rows, 128
        )
    pair_full = jnp.concatenate(
        [flat_all[:, i].reshape(columns * pair_rows, 128) for i in range(strips)], axis=1
    )
    query_full = early_all[:, :width]
    latent_full = early_all[:, width : width + features]
    output_full = early_all[:, width + features : 2 * width + features]

    rows = tokens.astype(F32)
    normed, first_scale = norm_forward(rows, first_gain)
    normed_block = gather_true(normed.astype(BF16))
    block = normed_block.shape[0]
    portion = block // 2
    mask = head_mask(width)
    spread = jnp.where(mask, jnp.concatenate([pair_full] * LATENT_HEADS, axis=0), jnp.zeros((), BF16))
    spread = near_features(spread, portion)
    latent_part = dot(normed_block, latent_full, 1, 0).astype(BF16)
    near, far, prompt_there, cot_block = gather_latents(latent_part, cotangent)
    scale = HEAD_DIM**-0.5
    queries_t = (dot(query_full, normed_block, 0, 1).astype(BF16) * scale).astype(BF16)
    queries = (dot(normed_block, query_full, 1, 0).astype(BF16) * scale).astype(BF16)
    meta = key_layout(block_order, portion)
    late, _ = together(late, prompt_there)
    queries_t, queries, cot_block = together(queries_t, queries, cot_block)
    late_all = lax.all_gather(late, "col", axis=0, tiled=True)
    wide_full = late_all[:, : 2 * units]
    down_full = late_all[:, 2 * units :]
    result_t, attended_t, lse = attend(meta, queries_t, near, far, spread, portion)
    branch = dot(attended_t, output_full, 0, 1)
    hidden = rows + scatter_true(branch)

    normed2, second_scale = norm_forward(hidden, second_gain)
    normed2_block = gather_near(normed2.astype(BF16))
    both = dot(normed2_block, wide_full, 1, 0)
    gate = both[:, :units]
    up = both[:, units:]
    sigma = jax.nn.sigmoid(gate)
    act = (gate * sigma * up).astype(BF16)
    act_grad = dot(cot_block, down_full, 1, 0)
    gate_grad = (act_grad * up * sigma * (1.0 + gate * (1.0 - sigma))).astype(BF16)
    up_grad = (act_grad * gate * sigma).astype(BF16)
    both_grad = jnp.concatenate([gate_grad, up_grad], axis=1)
    normed2_grad = scatter_near(dot(both_grad, wide_full, 1, 1))
    late_terms = jnp.concatenate(
        [
            dot(normed2_block, both_grad, 0, 0).astype(BF16),
            dot(cot_block, act, 0, 0).astype(BF16),
        ],
        axis=1,
    )
    late_terms, normed2_grad = together(late_terms, normed2_grad)
    late_sums = lax.psum_scatter(late_terms, "col", scatter_dimension=0, tiled=True).astype(F32)
    norm2_grad, second_gain_term = norm_backward(hidden, second_scale, second_gain, normed2_grad)
    hidden_grad = cotangent.astype(F32) + norm2_grad

    branch_block = gather_true(hidden_grad.astype(BF16))
    act, branch_block = lax.optimization_barrier((act, branch_block))
    layer = hidden + scatter_near(dot(act, down_full, 1, 1))
    attended_grad = dot(branch_block, output_full, 1, 0).astype(BF16)
    attended_grad_t = dot(output_full, branch_block, 0, 1).astype(BF16)
    inner = jnp.sum(
        (attended_grad_t.astype(F32) * result_t).reshape(-1, HEAD_DIM, block), axis=1
    )
    inner = jnp.pad(inner, ((0, 8 - inner.shape[0]), (0, 0)))
    query_grad_t, latent_terms, pair_big = attend_back(
        meta, queries_t, attended_grad_t, queries, attended_grad, lse, inner, near, far, spread,
        portion,
    )
    def column_terms():
        output_term = dot(branch_block, attended_t, 0, 1).astype(BF16)
        query_term = dot(normed_block, query_grad_t, 0, 1).astype(BF16)
        pair_table = near_features(pair_big, portion)
        pair_term = jnp.where(mask[:LATENT], pair_table[:LATENT], pair_table[LATENT:])
        pair_terms = pair_term.astype(BF16).reshape(columns, pair_rows, strips, 128)
        pair_terms = jnp.concatenate([pair_terms[:, :, i] for i in range(strips)], axis=1)
        pair_terms = jnp.pad(pair_terms, ((0, 0), (0, share - strips * pair_rows), (0, 0)))
        return jnp.concatenate(
            [query_term, output_term, pair_terms.reshape(columns * share, 128)], axis=1
        )

    latent_grad, early_sums = scatter_latents(latent_terms, portion, column_terms)
    pair_sums = early_sums[:, 2 * width :]
    latent_term = dot(normed_block, latent_grad, 0, 0).astype(BF16)
    norm_part = (
        dot(query_grad_t, query_full, 0, 1) + dot(latent_grad, latent_full, 1, 1)
    ).astype(BF16)
    if paired_columns(portion):
        mine, got = column_first(latent_term)
        pieces = true_pieces(norm_part)
        got, *first = together(got, *scatter_first(pieces))
        mine, got = column_second(mine, got)
        *got, low_last, high_last = together(*got, *scatter_second(pieces, *first))
        latent_sums = column_last(mine, got)
        normed_grad = scatter_last(pieces, *first, low_last, high_last)
    else:
        latent_sums = lax.psum_scatter(
            latent_term, "col", scatter_dimension=0, tiled=True
        ).astype(F32)
        normed_grad = scatter_true(norm_part)
    norm1_grad, first_gain_term = norm_backward(rows, first_scale, first_gain, normed_grad)
    input_gradient = hidden_grad + norm1_grad
    gains = all_sum(jnp.stack([first_gain_term, second_gain_term]))
    pair_sum = jnp.concatenate(
        [pair_sums[i * pair_rows : (i + 1) * pair_rows] for i in range(strips)], axis=1
    )
    return (
        layer,
        input_gradient,
        gains[0],
        early_sums[:, :width],
        latent_sums,
        pair_sum[:, :width],
        pair_sum[:, width:],
        early_sums[:, width : 2 * width].T,
        gains[1],
        late_sums[:, :hidden_units],
        late_sums[:, units : units + hidden_units],
        late_sums[:, 2 * units : 2 * units + hidden_units].T,
    )


def solution(mesh):
    rows = P(("col", "row"), None)
    placed = (
        rows, P(), P("col", "row"), P("col", "row"), P("col", "row"), P("col", "row"),
        P("row", "col"), P(), P("col", "row"), P("col", "row"), P("row", "col"), P(), rows,
    )
    given = (
        rows, rows, P(), P("col", "row"), P("col", "row"), P("col", "row"), P("col", "row"),
        P("row", "col"), P(), P("col", "row"), P("col", "row"), P("row", "col"),
    )
    return jax.shard_map(
        per_device, mesh=mesh, in_specs=placed, out_specs=given, check_vma=False
    )
```

```python
import functools

import jax
import jax.numpy as jnp
from jax import lax
from jax.experimental import pallas as pl
from jax.experimental.pallas import tpu as pltpu
from jax.sharding import PartitionSpec as P

HEAD_DIM = 64
LATENT_HEADS = 2
LATENT = 256
PROMPT = 4096
CONT = 512
KEY_TILE = 512
ROW_TILE = 256
TALL = HEAD_DIM + 16
LOG2E = 1.4426950408889634

epsilon = 1e-05
masked_value = -1e30
BF16 = jnp.bfloat16
F32 = jnp.float32


def dot(left, right, left_dim, right_dim):
    return lax.dot_general(
        left, right, (((left_dim,), (right_dim,)), ((), ())), preferred_element_type=F32
    )


def norm_forward(rows, gain):
    scale = lax.rsqrt(jnp.mean(rows * rows, axis=-1, keepdims=True) + epsilon)
    return (rows * scale * gain, scale)


def norm_backward(rows, scale, gain, grad_out):
    normal = rows * scale
    gain_term = jnp.sum(grad_out * normal, axis=0)
    inner = grad_out * gain
    grad_rows = scale * (inner - normal * jnp.mean(inner * normal, axis=-1, keepdims=True))
    return (grad_rows, gain_term)


def exchange(block, mask):
    return lax.ppermute(block, "row", [(i, i ^ mask) for i in range(lax.axis_size("row"))])


def together(*values):
    return lax.optimization_barrier(values)


def gather_first(rows):
    half = rows.shape[0] // 2
    return exchange(rows[:half], 1), exchange(rows[half:], 2)


def gather_second(rows, low_x, high_y):
    half = rows.shape[0] // 2
    low_y = exchange(jnp.concatenate([rows[:half], low_x], axis=0), 2)
    high_x = exchange(jnp.concatenate([rows[half:], high_y], axis=0), 1)
    return low_y, high_x


def gather_order(rows, low_x, high_y, low_y, high_x):
    half = rows.shape[0] // 2
    return [
        (rows[:half], rows[half:]),
        (low_x, high_x[:half]),
        (low_y[:half], high_y),
        (low_y[half:], high_x[half:]),
    ]


def gather_pieces(rows):
    first = together(*gather_first(rows))
    return gather_order(rows, *first, *together(*gather_second(rows, *first)))


def join(pieces):
    return jnp.concatenate([part for piece in pieces for part in piece], axis=0)


def gather_near(rows):
    if lax.axis_size("row") != 4:
        return lax.all_gather(rows, "row", axis=0, tiled=True)
    return join(gather_pieces(rows))


def gather_true(rows):
    if lax.axis_size("row") != 4:
        return lax.all_gather(rows, "row", axis=0, tiled=True)
    count = rows.shape[0]
    here = lax.axis_index("row")
    whole = jnp.zeros((4 * count,) + rows.shape[1:], rows.dtype)
    for j, piece in enumerate(gather_pieces(rows)):
        whole = lax.dynamic_update_slice_in_dim(
            whole, jnp.concatenate(piece, axis=0), (here ^ j) * count, 0
        )
    return whole


def scatter_first(pieces):
    half = pieces[0].shape[0] // 2
    return (
        exchange(jnp.concatenate([pieces[2][:half], pieces[3][:half]], axis=0), 2),
        exchange(jnp.concatenate([pieces[1][half:], pieces[3][half:]], axis=0), 1),
    )


def scatter_second(pieces, low_in, high_in):
    half = pieces[0].shape[0] // 2
    return (
        exchange(add_low(pieces[1][:half], low_in[half:]), 1),
        exchange(add_low(pieces[2][half:], high_in[half:]), 2),
    )


def scatter_last(pieces, low_in, high_in, low_last, high_last):
    half = pieces[0].shape[0] // 2
    low = pieces[0][:half].astype(F32) + low_in[:half].astype(F32) + low_last.astype(F32)
    high = pieces[0][half:].astype(F32) + high_in[:half].astype(F32) + high_last.astype(F32)
    return jnp.concatenate([low, high], axis=0)


def scatter_pieces(pieces):
    first = together(*scatter_first(pieces))
    return scatter_last(pieces, *first, *together(*scatter_second(pieces, *first)))


def add_low(left, right):
    return (left.astype(F32) + right.astype(F32)).astype(BF16)


def scatter_near(part):
    part = part.astype(BF16)
    if lax.axis_size("row") != 4:
        return lax.psum_scatter(part, "row", scatter_dimension=0, tiled=True).astype(F32)
    count = part.shape[0] // 4
    return scatter_pieces([part[j * count : (j + 1) * count] for j in range(4)])


def true_pieces(part):
    count = part.shape[0] // 4
    here = lax.axis_index("row")
    return [lax.dynamic_slice_in_dim(part, (here ^ j) * count, count, 0) for j in range(4)]


def scatter_true(part):
    part = part.astype(BF16)
    if lax.axis_size("row") != 4:
        return lax.psum_scatter(part, "row", scatter_dimension=0, tiled=True).astype(F32)
    return scatter_pieces(true_pieces(part))


def across(block, mask):
    return lax.ppermute(block, "col", [(i, i ^ mask) for i in range(lax.axis_size("col"))])


def column_first(part):
    size = lax.axis_size("col")
    count = part.shape[0] // size
    here = lax.axis_index("col")

    def pieces(order):
        return jnp.concatenate(
            [lax.dynamic_slice_in_dim(part, (here ^ j) * count, count, 0) for j in order], axis=0
        )

    return pieces((0, 2, 4, 6)), across(pieces((1, 3, 5, 7)), 1)


def column_second(mine, got):
    count = mine.shape[0] // 4
    mine = mine.astype(F32) + got.astype(F32)
    low = mine.astype(BF16)
    return mine[:count], [across(low[j * count : (j + 1) * count], 2 * j) for j in (1, 2, 3)]


def column_last(mine, got):
    return (mine + got[0].astype(F32)) + (got[1].astype(F32) + got[2].astype(F32))


def all_sum(value):
    if lax.axis_size("row") == 4 and lax.axis_size("col") == 8:
        value = (value + exchange(value, 1)) + (exchange(value, 2) + exchange(value, 3))
        value = value + across(value, 1)
        return (value + across(value, 2)) + (across(value, 4) + across(value, 6))
    return lax.psum(value, ("row", "col"))


def masked_heads(tile, heads):
    lanes = lax.broadcasted_iota(jnp.int32, tile.shape, 1) // HEAD_DIM
    return [jnp.where(lanes == h, tile, jnp.zeros_like(tile)) for h in range(heads)]


def one_head(ref, h, rows):
    pair = pl.ds((h // 2) * 2 * HEAD_DIM, 2 * HEAD_DIM)
    own = ref[h * HEAD_DIM : (h + 1) * HEAD_DIM, rows]
    none = jnp.zeros_like(own)
    return pair, jnp.concatenate([own, none] if h % 2 == 0 else [none, own], axis=0)


def visit_tiles(meta, step, prompt_tiles, portion, rows, body):
    place = meta[prompt_tiles + portion // KEY_TILE]
    first_rows = portion // ROW_TILE

    def visit(index, carry):
        is_prompt = index < first_rows
        row0 = index * ROW_TILE
        position = place * portion + row0
        later = row0 - portion
        key0 = step * KEY_TILE
        on_prompt = step < prompt_tiles
        prompt_full = is_prompt & on_prompt & (key0 + KEY_TILE - 1 <= position)
        prompt_part = is_prompt & on_prompt & (key0 <= position + ROW_TILE - 1)
        full = prompt_full | (jnp.logical_not(is_prompt) & on_prompt)
        own_part = (
            jnp.logical_not(is_prompt)
            & jnp.logical_not(on_prompt)
            & (later // CONT == step - prompt_tiles)
        )
        partly = (prompt_part & jnp.logical_not(prompt_full)) | own_part
        ahead = jnp.where(is_prompt, position - key0, later % CONT)

        @pl.when(full)
        def _():
            body(index, None, KEY_TILE)

        @pl.when(partly & (ahead < ROW_TILE))
        def _():
            body(index, ahead, ROW_TILE)

        @pl.when(partly & (ahead >= ROW_TILE))
        def _():
            body(index, ahead, KEY_TILE)

        return carry

    lax.fori_loop(0, rows // ROW_TILE, visit, 0)


def hide(scores, ahead):
    if ahead is None:
        return scores
    key = lax.broadcasted_iota(jnp.int32, scores.shape, 0)
    query = lax.broadcasted_iota(jnp.int32, scores.shape, 1)
    return jnp.where(key <= query + ahead, scores, masked_value)


def load_pairs(step, near_tiles, meta, near, far, spread, latents):
    place = meta[step]

    @pl.when(place < near_tiles)
    def _():
        latents[...] = jnp.concatenate([near[j] for j in range(near.shape[0])], axis=1)

    @pl.when(place >= near_tiles)
    def _():
        latents[...] = jnp.concatenate([far[j] for j in range(far.shape[0])], axis=1)

    return dot(latents[...], spread[...], 1, 0).astype(BF16)


def attend_kernel(
    meta, q_t, near, far, spread, out, out_low, lse, latents, keys, values_t, acc, top, total,
    *, heads, prompt_tiles, near_tiles, portion, rows,
):
    step = pl.program_id(0)
    width = heads * HEAD_DIM

    @pl.when(step == 0)
    def _():
        acc[...] = jnp.zeros_like(acc)
        top[...] = jnp.full_like(top, masked_value)
        total[...] = jnp.zeros_like(total)
        values_t[...] = jnp.ones_like(values_t)

    pairs = load_pairs(step, near_tiles, meta, near, far, spread, latents)
    keys[...] = pairs[:, :width]
    turned = pairs[:, width:].T
    for h in range(heads):
        values_t[h * TALL : h * TALL + HEAD_DIM, :] = turned[h * HEAD_DIM : (h + 1) * HEAD_DIM]

    def body(index, ahead, count):
        at = pl.ds(pl.multiple_of(index * ROW_TILE, ROW_TILE), ROW_TILE)
        before = top[:, at]
        sums = total[:, at]
        nows = []
        news = []
        results = []
        for first in range(0, heads, 2):
            scores = []
            for h in (first, first + 1):
                pair, query = one_head(q_t, h, at)
                scores.append(hide(dot(keys[:count, pair], query, 1, 0), ahead))
            for h in (first, first + 1):
                score = scores[h - first]
                now = jnp.maximum(before[h : h + 1], jnp.max(score, axis=0, keepdims=True))
                probs = jnp.exp2(score - now).astype(BF16)
                decay = jnp.exp2(before[h : h + 1] - now)
                got = dot(values_t[h * TALL : (h + 1) * TALL, :count], probs, 1, 0)
                nows.append(now)
                news.append(decay * sums[h : h + 1] + got[HEAD_DIM : HEAD_DIM + 1])
                mine = slice(h * HEAD_DIM, (h + 1) * HEAD_DIM)
                results.append(decay * acc[mine, at] + got[:HEAD_DIM])
        for h in range(heads):
            top[h : h + 1, at] = nows[h]
            total[h : h + 1, at] = news[h]
            acc[h * HEAD_DIM : (h + 1) * HEAD_DIM, at] = results[h]

    visit_tiles(meta, step, prompt_tiles, portion, rows, body)

    @pl.when(step == pl.num_programs(0) - 1)
    def _():
        lse[...] = top[...] + jnp.log2(jnp.maximum(total[...], 1e-37))
        for h in range(heads):
            mine = slice(h * HEAD_DIM, (h + 1) * HEAD_DIM)
            result = acc[mine, :] / total[h : h + 1, :]
            out[mine, :] = result
            out_low[mine, :] = result.astype(BF16)


def attend_back_kernel(
    meta, q_t, grad_t, q, grad, lse, inner, near, far, spread,
    query_grad, latent_grad, pair_grad,
    latents, keys, keys_t, values, queries_apart, grads_apart, query_acc, key_acc, value_acc,
    *, heads, prompt_tiles, near_tiles, portion, rows,
):
    step = pl.program_id(0)
    tall = heads * ROW_TILE
    width = heads * HEAD_DIM

    @pl.when(step == 0)
    def _():
        query_acc[...] = jnp.zeros_like(query_acc)
        pair_grad[...] = jnp.zeros_like(pair_grad)

        def apart(index, carry):
            at = pl.ds(pl.multiple_of(index * ROW_TILE, ROW_TILE), ROW_TILE)
            to = pl.ds(pl.multiple_of(index * tall, tall), tall)
            queries_apart[to, :] = jnp.concatenate(masked_heads(q[at, :], heads), axis=0)
            grads_apart[to, :] = jnp.concatenate(masked_heads(grad[at, :], heads), axis=0)
            return carry

        lax.fori_loop(0, rows // ROW_TILE, apart, 0)

    key_acc[...] = jnp.zeros_like(key_acc)
    value_acc[...] = jnp.zeros_like(value_acc)
    pairs = load_pairs(step, near_tiles, meta, near, far, spread, latents)
    keys[...] = pairs[:, :width]
    keys_t[...] = pairs[:, :width].T
    values[...] = pairs[:, width:]

    def body(index, ahead, count):
        at = pl.ds(pl.multiple_of(index * ROW_TILE, ROW_TILE), ROW_TILE)
        to = pl.ds(pl.multiple_of(index * tall, tall), tall)
        all_probs = []
        all_grads = []
        for h in range(heads):
            pair, query = one_head(q_t, h, at)
            _, out_grad = one_head(grad_t, h, at)
            scores = hide(dot(keys[:count, pair], query, 1, 0), ahead)
            probs = jnp.exp2(scores - lse[h : h + 1, at])
            dprobs = dot(values[:count, pair], out_grad, 1, 0)
            score_grad = (probs * (dprobs - inner[h : h + 1, at])).astype(BF16)
            mine = slice(h * HEAD_DIM, (h + 1) * HEAD_DIM)
            query_acc[mine, at] += dot(keys_t[mine, :count], score_grad, 1, 0)
            all_probs.append(probs.astype(BF16))
            all_grads.append(score_grad)
        value_acc[:count] += dot(jnp.concatenate(all_probs, axis=1), grads_apart[to, :], 1, 0)
        key_acc[:count] += dot(jnp.concatenate(all_grads, axis=1), queries_apart[to, :], 1, 0)

    visit_tiles(meta, step, prompt_tiles, portion, rows, body)

    pair_low = jnp.concatenate([key_acc[...].astype(BF16), value_acc[...].astype(BF16)], axis=1)
    grads = dot(pair_low, spread[...], 1, 1).astype(BF16)
    for j in range(latent_grad.shape[0]):
        latent_grad[j] = grads[:, j * 128 : (j + 1) * 128]
    pair_grad[...] += dot(latents[...], pair_low, 0, 0)

    @pl.when(step == pl.num_programs(0) - 1)
    def _():
        query_grad[...] = (query_acc[...] * HEAD_DIM**-0.5).astype(BF16)


def whole_spec(shape):
    return pl.BlockSpec(shape, lambda step, meta: (0, 0))


def latent_specs(near, far, spread):
    near_tiles = near.shape[1] // KEY_TILE
    tile = (near.shape[0], KEY_TILE, 128)
    return [
        pl.BlockSpec(tile, lambda step, meta: (0, jnp.minimum(meta[step], near_tiles - 1), 0)),
        pl.BlockSpec(tile, lambda step, meta: (0, jnp.maximum(meta[step] - near_tiles, 0), 0)),
        whole_spec(spread.shape),
    ]


def attend(meta, q_t, near, far, spread, portion):
    width, rows = q_t.shape
    heads = width // HEAD_DIM
    prompt_tiles = PROMPT // KEY_TILE
    steps = prompt_tiles + portion // KEY_TILE
    keys = (PROMPT + portion) * rows * heads * 3 // 4
    return pl.pallas_call(
        functools.partial(
            attend_kernel, heads=heads, prompt_tiles=prompt_tiles,
            near_tiles=near.shape[1] // KEY_TILE, portion=portion, rows=rows,
        ),
        grid_spec=pltpu.PrefetchScalarGridSpec(
            num_scalar_prefetch=1,
            grid=(steps,),
            in_specs=[whole_spec((width, rows))] + latent_specs(near, far, spread),
            out_specs=[
                whole_spec((width, rows)),
                whole_spec((width, rows)),
                whole_spec((8, rows)),
            ],
            scratch_shapes=[
                pltpu.VMEM((KEY_TILE, spread.shape[0]), BF16),
                pltpu.VMEM((KEY_TILE, width), BF16),
                pltpu.VMEM((heads * TALL, KEY_TILE), BF16),
                pltpu.VMEM((width, rows), F32),
                pltpu.VMEM((8, rows), F32),
                pltpu.VMEM((8, rows), F32),
            ],
        ),
        out_shape=[
            jax.ShapeDtypeStruct((width, rows), F32),
            jax.ShapeDtypeStruct((width, rows), BF16),
            jax.ShapeDtypeStruct((8, rows), F32),
        ],
        compiler_params=pltpu.CompilerParams(dimension_semantics=("arbitrary",)),
        cost_estimate=pl.CostEstimate(
            flops=keys * HEAD_DIM * 16, transcendentals=keys, bytes_accessed=8 << 20
        ),
        name="attend",
    )(meta, q_t, near, far, spread)


def attend_back(meta, q_t, grad_t, q, grad, lse, inner, near, far, spread, portion):
    width, rows = q_t.shape
    heads = width // HEAD_DIM
    planes = near.shape[0]
    features = spread.shape[0]
    prompt_tiles = PROMPT // KEY_TILE
    steps = prompt_tiles + portion // KEY_TILE
    keys = (PROMPT + portion) * rows * heads * 3 // 4
    return pl.pallas_call(
        functools.partial(
            attend_back_kernel, heads=heads, prompt_tiles=prompt_tiles,
            near_tiles=near.shape[1] // KEY_TILE, portion=portion, rows=rows,
        ),
        grid_spec=pltpu.PrefetchScalarGridSpec(
            num_scalar_prefetch=1,
            grid=(steps,),
            in_specs=[
                whole_spec((width, rows)),
                whole_spec((width, rows)),
                whole_spec((rows, width)),
                whole_spec((rows, width)),
                whole_spec((8, rows)),
                whole_spec((8, rows)),
            ]
            + latent_specs(near, far, spread),
            out_specs=[
                whole_spec((width, rows)),
                pl.BlockSpec((planes, KEY_TILE, 128), lambda step, meta: (0, meta[step], 0)),
                whole_spec((features, 2 * width)),
            ],
            scratch_shapes=[
                pltpu.VMEM((KEY_TILE, features), BF16),
                pltpu.VMEM((KEY_TILE, width), BF16),
                pltpu.VMEM((width, KEY_TILE), BF16),
                pltpu.VMEM((KEY_TILE, width), BF16),
                pltpu.VMEM((heads * rows, width), BF16),
                pltpu.VMEM((heads * rows, width), BF16),
                pltpu.VMEM((width, rows), F32),
                pltpu.VMEM((KEY_TILE, width), F32),
                pltpu.VMEM((KEY_TILE, width), F32),
            ],
        ),
        out_shape=[
            jax.ShapeDtypeStruct((width, rows), BF16),
            jax.ShapeDtypeStruct((planes, PROMPT + portion, 128), BF16),
            jax.ShapeDtypeStruct((features, 2 * width), F32),
        ],
        compiler_params=pltpu.CompilerParams(dimension_semantics=("arbitrary",)),
        cost_estimate=pl.CostEstimate(
            flops=keys * HEAD_DIM * 40, transcendentals=keys, bytes_accessed=14 << 20
        ),
        name="attend_back",
    )(meta, q_t, grad_t, q, grad, lse, inner, near, far, spread)


def paired_columns(portion):
    return (
        lax.axis_size("row") == 4 and lax.axis_size("col") == 8 and PROMPT // portion == 8
    )


def key_layout(block_order, portion):
    portions = PROMPT // portion
    column = lax.axis_index("col")
    base = column // portions * portions
    ident = block_order[column]
    group = ident // portions
    place = ident % portions
    slots = jnp.arange(block_order.shape[0], dtype=jnp.int32)
    parts = group * portions + jnp.arange(portions, dtype=jnp.int32)
    sources = jnp.sum(jnp.where(block_order[None, :] == parts[:, None], slots[None, :], 0), axis=1)
    split = portion // KEY_TILE
    prompt_tiles = portions * split
    if paired_columns(portion):
        apart = sources ^ column
        tiles = jnp.where(apart % 2 == 0, apart // 2, 5 + apart // 2)
        own = jnp.full((1,), 4, jnp.int32)
    else:
        tiles = (sources - base)[:, None] * split + jnp.arange(split, dtype=jnp.int32)[None, :]
        own = prompt_tiles + jnp.arange(split, dtype=jnp.int32)
    return jnp.concatenate([tiles.reshape(-1), own, place[None]]).astype(jnp.int32)


def bit_of(value, bit):
    return value // (1 << bit) % 2


def swapped(block, axis, distance):
    size = lax.axis_size(axis)
    return lax.ppermute(block, axis, [(i, i ^ 1 << distance) for i in range(size)])


def gather_prompt(held):
    portion = held.shape[0]
    portions = PROMPT // portion
    if portions == lax.axis_size("col"):
        return lax.all_gather(held, "col", axis=0, tiled=True)
    column = lax.axis_index("col")
    for bit in range(portions.bit_length() - 1):
        other = swapped(held, "col", bit)
        upper = bit_of(column, bit) == 1
        held = jnp.where(
            upper, jnp.concatenate([other, held], axis=0), jnp.concatenate([held, other], axis=0)
        )
    return held


def scatter_prompt(buffer, portion):
    portions = PROMPT // portion
    if portions == lax.axis_size("col"):
        return lax.psum_scatter(buffer, "col", scatter_dimension=0, tiled=True)
    column = lax.axis_index("col")
    for bit in reversed(range(portions.bit_length() - 1)):
        half = buffer.shape[0] // 2
        upper = bit_of(column, bit) == 1
        keep = jnp.where(upper, buffer[half:], buffer[:half])
        outgoing = jnp.where(upper, buffer[:half], buffer[half:])
        got = swapped(outgoing, "col", bit)
        buffer = (keep.astype(F32) + got.astype(F32)).astype(BF16)
    return buffer


def planes_of(whole):
    return jnp.stack([whole[:, j : j + 128] for j in range(0, whole.shape[1], 128)], axis=0)


def gather_latents(part, beside):
    portion = part.shape[0] // 2
    if not paired_columns(portion):
        whole = lax.all_gather(part, "row", axis=1, tiled=True)
        near = planes_of(gather_prompt(whole[:portion]))
        return near, planes_of(whole[portion:]), near[:, :8], gather_near(beside)
    held = part[:portion]
    beside, held = together(beside, held)
    first = gather_first(beside)
    got = together(*[across(held, mask) for mask in (2, 4, 6)], *first)
    *got, low_x, high_y = got
    held = jnp.concatenate([held, *got, part[portion:]], axis=0)
    beside = join(
        gather_order(beside, low_x, high_y, *together(*gather_second(beside, low_x, high_y)))
    )
    near = jnp.stack([jnp.concatenate(piece, axis=0) for piece in gather_pieces(held)], axis=0)
    return near, across(near[:, : 4 * portion], 1), got[0], beside


def scatter_latents(grad, portion):
    if not paired_columns(portion):
        whole = jnp.concatenate([grad[j] for j in range(grad.shape[0])], axis=1)
        prompt = scatter_prompt(whole[:PROMPT], portion)
        whole = jnp.concatenate([prompt, whole[PROMPT:]], axis=0)
        return lax.psum_scatter(whole, "row", scatter_dimension=1, tiled=True)
    here = 4 * portion
    got = across(grad[:, here + portion :], 1)
    pieces = [
        jnp.concatenate(
            [add_low(grad[j, :here], got[j]), grad[j, here : here + portion]], axis=0
        )
        for j in range(4)
    ]
    mine = scatter_pieces(pieces)
    low = mine[:here].astype(BF16)
    got = together(
        *[across(low[j * portion : (j + 1) * portion], 2 * j) for j in (1, 2, 3)]
    )
    prompt = (mine[:portion] + got[0].astype(F32)) + (got[1].astype(F32) + got[2].astype(F32))
    return jnp.concatenate([prompt.astype(BF16), mine[here:].astype(BF16)], axis=0)


def near_features(table, portion):
    if not paired_columns(portion):
        return table
    here = lax.axis_index("row")
    count = table.shape[0] // 4
    return jnp.concatenate(
        [lax.dynamic_slice_in_dim(table, (here ^ j) * count, count, 0) for j in range(4)], axis=0
    )


def padded(block, width):
    return jnp.pad(block, ((0, 0), (0, width - block.shape[1])))


def head_mask(width):
    group = lax.broadcasted_iota(jnp.int32, (LATENT_HEADS * LATENT, 2 * width), 0) // LATENT
    head = lax.broadcasted_iota(jnp.int32, (LATENT_HEADS * LATENT, 2 * width), 1) // HEAD_DIM
    return group == head % LATENT_HEADS


def per_device(
    tokens, first_gain, query_weight, latent_weight, key_weight, value_weight, output_weight,
    second_gain, gate_weight, up_weight, down_weight, block_order, cotangent,
):
    columns = lax.axis_size("col")
    share = query_weight.shape[0]
    width = query_weight.shape[1]
    features = latent_weight.shape[1]
    hidden_units = gate_weight.shape[1]
    units = -(-hidden_units // 128) * 128

    early = jnp.concatenate(
        [query_weight, latent_weight, output_weight.T], axis=1
    )
    pair_weight = jnp.concatenate([key_weight, value_weight], axis=1)
    late = jnp.concatenate(
        [padded(gate_weight, units), padded(up_weight, units), padded(down_weight.T, units)], axis=1
    )
    pair_rows = pair_weight.shape[0]
    strips = 2 * width // 128
    pair_flat = jnp.concatenate(
        [pair_weight[:, i * 128 : (i + 1) * 128] for i in range(strips)], axis=0
    )
    if pair_flat.shape[0] == share:
        early_all = lax.all_gather(
            jnp.concatenate([early, pair_flat], axis=1), "col", axis=0, tiled=True
        )
        flat_all = early_all[:, early.shape[1] :].reshape(columns, strips, pair_rows, 128)
    else:
        early_all = lax.all_gather(early, "col", axis=0, tiled=True)
        flat_all = lax.all_gather(pair_flat, "col", axis=0, tiled=True).reshape(
            columns, strips, pair_rows, 128
        )
    pair_full = jnp.concatenate(
        [flat_all[:, i].reshape(columns * pair_rows, 128) for i in range(strips)], axis=1
    )
    query_full = early_all[:, :width]
    latent_full = early_all[:, width : width + features]
    output_full = early_all[:, width + features : 2 * width + features]

    rows = tokens.astype(F32)
    normed, first_scale = norm_forward(rows, first_gain)
    normed_block = gather_true(normed.astype(BF16))
    block = normed_block.shape[0]
    portion = block // 2
    mask = head_mask(width)
    spread = jnp.where(mask, jnp.concatenate([pair_full] * LATENT_HEADS, axis=0), jnp.zeros((), BF16))
    spread = near_features(spread, portion)
    latent_part = dot(normed_block, latent_full, 1, 0).astype(BF16)
    near, far, prompt_there, cot_block = gather_latents(latent_part, cotangent)
    scale = HEAD_DIM**-0.5
    queries_t = (dot(query_full, normed_block, 0, 1) * (scale * LOG2E)).astype(BF16)
    queries = (dot(normed_block, query_full, 1, 0).astype(BF16) * scale).astype(BF16)
    meta = key_layout(block_order, portion)
    late, _ = together(late, prompt_there)
    queries_t, queries, cot_block = together(queries_t, queries, cot_block)
    late_all = lax.all_gather(late, "col", axis=0, tiled=True)
    wide_full = late_all[:, : 2 * units]
    down_full = late_all[:, 2 * units :]
    result_t, attended_t, lse = attend(meta, queries_t, near, far, spread, portion)
    branch = dot(attended_t, output_full, 0, 1)
    hidden = rows + scatter_true(branch)

    normed2, second_scale = norm_forward(hidden, second_gain)
    normed2_block = gather_near(normed2.astype(BF16))
    both = dot(normed2_block, wide_full, 1, 0)
    gate = both[:, :units]
    up = both[:, units:]
    sigma = jax.nn.sigmoid(gate)
    act = (gate * sigma * up).astype(BF16)
    act_grad = dot(cot_block, down_full, 1, 0)
    gate_grad = (act_grad * up * sigma * (1.0 + gate * (1.0 - sigma))).astype(BF16)
    up_grad = (act_grad * gate * sigma).astype(BF16)
    both_grad = jnp.concatenate([gate_grad, up_grad], axis=1)
    normed2_grad = scatter_near(dot(both_grad, wide_full, 1, 1))
    late_terms = jnp.concatenate(
        [
            dot(normed2_block, both_grad, 0, 0).astype(BF16),
            dot(cot_block, act, 0, 0).astype(BF16),
        ],
        axis=1,
    )
    late_terms, normed2_grad = together(late_terms, normed2_grad)
    late_sums = lax.psum_scatter(late_terms, "col", scatter_dimension=0, tiled=True).astype(F32)
    norm2_grad, second_gain_term = norm_backward(hidden, second_scale, second_gain, normed2_grad)
    hidden_grad = cotangent.astype(F32) + norm2_grad

    branch_block = gather_true(hidden_grad.astype(BF16))
    act, branch_block = lax.optimization_barrier((act, branch_block))
    layer = hidden + scatter_near(dot(act, down_full, 1, 1))
    attended_grad = dot(branch_block, output_full, 1, 0).astype(BF16)
    attended_grad_t = dot(output_full, branch_block, 0, 1).astype(BF16)
    inner = jnp.sum(
        (attended_grad_t.astype(F32) * result_t).reshape(-1, HEAD_DIM, block), axis=1
    )
    inner = jnp.pad(inner, ((0, 8 - inner.shape[0]), (0, 0)))
    query_grad_t, latent_terms, pair_big = attend_back(
        meta, queries_t, attended_grad_t, queries, attended_grad, lse, inner, near, far, spread,
        portion,
    )
    latent_grad = scatter_latents(latent_terms, portion)
    output_term = dot(branch_block, attended_t, 0, 1).astype(BF16)
    query_term = dot(normed_block, query_grad_t, 0, 1).astype(BF16)
    pair_table = near_features(pair_big, portion)
    pair_term = jnp.where(mask[:LATENT], pair_table[:LATENT], pair_table[LATENT:])
    pair_terms = pair_term.astype(BF16).reshape(columns, pair_rows, strips, 128)
    pair_terms = jnp.concatenate([pair_terms[:, :, i] for i in range(strips)], axis=1)
    pair_terms = jnp.pad(pair_terms, ((0, 0), (0, share - strips * pair_rows), (0, 0)))
    early_terms = jnp.concatenate(
        [query_term, output_term, pair_terms.reshape(columns * share, 128)], axis=1
    )
    early_sums = lax.psum_scatter(early_terms, "col", scatter_dimension=0, tiled=True).astype(F32)
    pair_sums = early_sums[:, 2 * width :]
    latent_term = dot(normed_block, latent_grad, 0, 0).astype(BF16)
    norm_part = dot(query_grad_t, query_full, 0, 1) + dot(latent_grad, latent_full, 1, 1)
    first_gain_term = jnp.sum(norm_part * normed_block.astype(F32), axis=0) / first_gain
    norm_part = norm_part.astype(BF16)
    gains = jnp.stack([first_gain_term, second_gain_term])
    if paired_columns(portion):
        mine, got = column_first(latent_term)
        pieces = true_pieces(norm_part)
        got, *first = together(got, *scatter_first(pieces))
        mine, got = column_second(mine, got)
        *got, low_last, high_last = together(*got, *scatter_second(pieces, *first))
        latent_sums = column_last(mine, got)
        normed_grad = scatter_last(pieces, *first, low_last, high_last)
    else:
        latent_sums = lax.psum_scatter(
            latent_term, "col", scatter_dimension=0, tiled=True
        ).astype(F32)
        normed_grad = scatter_true(norm_part)
    gains = all_sum(gains)
    norm1_grad = norm_backward(rows, first_scale, first_gain, normed_grad)[0]
    input_gradient = hidden_grad + norm1_grad
    pair_sum = jnp.concatenate(
        [pair_sums[i * pair_rows : (i + 1) * pair_rows] for i in range(strips)], axis=1
    )
    return (
        layer,
        input_gradient,
        gains[0],
        early_sums[:, :width],
        latent_sums,
        pair_sum[:, :width],
        pair_sum[:, width:],
        early_sums[:, width : 2 * width].T,
        gains[1],
        late_sums[:, :hidden_units],
        late_sums[:, units : units + hidden_units],
        late_sums[:, 2 * units : 2 * units + hidden_units].T,
    )


def solution(mesh):
    rows = P(("col", "row"), None)
    placed = (
        rows, P(), P("col", "row"), P("col", "row"), P("col", "row"), P("col", "row"),
        P("row", "col"), P(), P("col", "row"), P("col", "row"), P("row", "col"), P(), rows,
    )
    given = (
        rows, rows, P(), P("col", "row"), P("col", "row"), P("col", "row"), P("col", "row"),
        P("row", "col"), P(), P("col", "row"), P("col", "row"), P("row", "col"),
    )
    return jax.shard_map(
        per_device, mesh=mesh, in_specs=placed, out_specs=given, check_vma=False
    )
```
